32 devices in a mesh: pairs: 8 (over y, x, core), rep: 4 (over z).
Axes of the slice: x: 2, y: 2, z: 4, core: 2. Of those that a mesh axis runs over, the one named last changes fastest.
Arguments:
- mat_val: bfloat16 [8192, 2048], P('pairs', 'rep'), may hold values from -6 to 6
- mat_cond: bfloat16 [1024, 2048], P('pairs', 'rep'), may hold values from -0.25 to 0.25
- screening: float32 [2048], P('rep'), may hold values from 0.2 to 2
- trial_cols: bfloat16 [1024, 256], P('pairs', 'rep'), may hold values from -0.09375 to 0.09375
- trial_rows: bfloat16 [8192, 256], P('pairs', 'rep'), may hold values from -6 to 6
- row_map: int32 [8192], replicated, may hold values from 0 to 8191, as said below
- val_index: int32 [8192], P('pairs'), may hold values from 0 to 127
- cond_index: int32 [8192], P('pairs'), may hold values from 0 to 255
- val_energy: float32 [128], replicated, may hold values from -1.5 to -0.25
- cond_energy: float32 [256], replicated, may hold values from 0.25 to 1.5
Outputs:
- response: bfloat16 [8192, 256], P('pairs', 'rep')
- kernel_tiles: bfloat16 [4, 8192, 1024], P('rep', 'pairs')
The draws below stay inside these ranges and needn't reach their ends.
Inputs may be any that keep to these rules, and one draw needn't show every extreme that they name: row_map is a permutation of the rows; of the 1024 rows of each aligned block, exactly 128 have values in each aligned block of 1024 values.
All inputs are finite; a program needn't handle non-finite values.
Results may differ from the reference program's by a relative error of at most 0.005.
Values may be sent and summed in bfloat16 or wider, within the bound.
No kernel may reach another device: no remote copies, remote signals or barrier semaphores. Data moves between devices by JAX's collectives and lax.ppermute only.
A program may use at most 64 MiB of HBM per device.

```python
import math
import jax
import jax.numpy as jnp
from jax import lax

G = 2048
NV = 256
NBV = 128
NBC = 256
P_DEV = 1024
ROWS = 8192
NCOL = 1024
PER_PEER = 128
G_SLICE = 512
SLICES = 4


def draw_row_map(key, part):
    device_count = ROWS // P_DEV
    first_key, second_key = jax.random.split(jax.random.fold_in(key, 7))
    sigma = jax.vmap(lambda subkey: jax.random.permutation(subkey, P_DEV))(jax.random.split(first_key, device_count))
    target = sigma // PER_PEER
    within = sigma % PER_PEER
    source_ids = jnp.arange(device_count, dtype=jnp.int32)[:, None]
    slot_before = source_ids * PER_PEER + within
    shuffle = jax.vmap(lambda subkey: jax.random.permutation(subkey, P_DEV))(jax.random.split(second_key, device_count))
    slot_after = shuffle[target, slot_before]
    return (target * P_DEV + slot_after).reshape(-1).astype(jnp.int32)


def plant(result, own_key, low, largest):
    index_at = [jax.random.randint(jax.random.fold_in(own_key, axis), (), 0, length) for axis, length in enumerate(result.shape)]
    longest = result.shape.index(max(result.shape))
    next_to = index_at[:longest] + [(index_at[longest] + 1) % result.shape[longest]] + index_at[longest + 1:]
    return result.at[tuple(index_at)].set(low).at[tuple(next_to)].set(largest)


def level_of(stream_key, extent, pieces, least, largest):
    level, own = 1.0, jax.random.fold_in(stream_key, 6)
    for axis_at, parts in pieces:
        steps = jnp.exp(jax.random.uniform(jax.random.fold_in(own, axis_at), (parts,), jnp.float32, least / len(pieces), largest / len(pieces)))
        level = level * jnp.repeat(steps, extent[axis_at] // parts).reshape([-1 if axis == axis_at else 1 for axis in range(len(extent))])
    return level


def noise(stream_key, dims, width, bound, shards=(), kind=jnp.bfloat16):
    result = jax.random.normal(stream_key, dims, jnp.float32) * width
    if len(shards) > 0:
        result = level_of(stream_key, dims, shards, -0.22, 0.18) * result
    return jnp.clip(result, min=-bound, max=bound).astype(kind)


def setup_inputs(seed: int = 0) -> dict:
    arg_keys = jax.random.split(jax.random.key(seed), 11)
    mat_val = noise(arg_keys[0], (ROWS, G), 1.0, 6.0, ((0, 8), (1, 4)))
    mat_cond = noise(arg_keys[1], (NCOL, G), G_SLICE ** -0.5, 0.25, ((0, 8), (1, 4)))
    screening = jnp.clip(jnp.exp(math.log(2.0) - 2.3025851 * jax.random.uniform(arg_keys[2], (G,), jnp.float32) ** level_of(arg_keys[2], (G,), ((0, 4),), -0.2, 0.2)), 0.2, 2.0)
    trial_cols = noise(arg_keys[3], (NCOL, NV), (NCOL * SLICES) ** -0.5, 0.09375, ((0, 8), (1, 4)))
    trial_rows = noise(arg_keys[4], (ROWS, NV), 1.0, 6.0, ((0, 8), (1, 4)))
    row_map = draw_row_map(jax.random.fold_in(arg_keys[10], 71), 0)
    val_index = plant(jax.random.randint(arg_keys[6], (ROWS,), 0, NBV), jax.random.fold_in(arg_keys[6], 1), 0, NBV - 1).astype(jnp.int32)
    cond_index = plant(jax.random.randint(arg_keys[7], (ROWS,), 0, NBC), jax.random.fold_in(arg_keys[7], 1), 0, NBC - 1).astype(jnp.int32)
    val_energy = jnp.clip(jax.random.uniform(arg_keys[8], (NBV,), jnp.float32, -1.5, -0.25), -1.5, -0.25)
    cond_energy = jnp.clip(jax.random.uniform(arg_keys[9], (NBC,), jnp.float32, 0.25, 1.5), 0.25, 1.5)
    return dict(mat_val=mat_val, mat_cond=mat_cond, screening=screening, trial_cols=trial_cols, trial_rows=trial_rows, row_map=row_map, val_index=val_index, cond_index=cond_index, val_energy=val_energy, cond_energy=cond_energy)


def reference(mat_val, mat_cond, screening, trial_cols, trial_rows, row_map, val_index, cond_index, val_energy, cond_energy):
    scaled = (mat_val.astype(jnp.float32) * screening[None, :]).astype(jnp.bfloat16)

    def one_slice(slice_idx):
        low_col = (slice_idx * G_SLICE).astype(jnp.int32)
        val_part = lax.dynamic_slice_in_dim(scaled, low_col, G_SLICE, 1)
        cond_part = lax.dynamic_slice_in_dim(mat_cond, low_col, G_SLICE, 1)

        def one_block(row_block):
            kernel_tile = lax.dot_general(row_block, cond_part, (((1,), (1,)), ((), ())), preferred_element_type=jnp.float32).astype(jnp.bfloat16)
            return kernel_tile, jnp.dot(kernel_tile, trial_cols, preferred_element_type=jnp.float32)

        tiles, contribution = lax.map(one_block, val_part.reshape(ROWS // P_DEV, P_DEV, G_SLICE))
        return tiles.reshape(ROWS, NCOL), contribution.reshape(ROWS, NV)

    kernel_tiles, contributions = lax.map(one_slice, jnp.arange(SLICES, dtype=jnp.int32))
    applied = jnp.sum(contributions, axis=0)
    inverse = jnp.argsort(row_map, stable=True).astype(jnp.int32)
    regrouped = applied[inverse]
    gap_values = cond_energy[cond_index] - val_energy[val_index]
    response = (gap_values[:, None] * trial_rows.astype(jnp.float32) + regrouped).astype(jnp.bfloat16)
    return response, kernel_tiles
```

```python
import functools
import jax
import jax.numpy as jnp
from jax import lax
from jax.experimental import pallas as pl
from jax.experimental.pallas import tpu as pltpu
from jax.sharding import PartitionSpec as P

F32 = jnp.float32
BF16 = jnp.bfloat16


def exchange(x, axis, mask):
    size = lax.axis_size(axis)
    return lax.ppermute(x, axis, [(i, i ^ mask) for i in range(size)])


def pair_gather(x):
    n = lax.axis_size("pairs")
    even = jnp.stack([x] + [exchange(x, "pairs", k) for k in range(2, n, 2)])
    odd = exchange(even, "pairs", 1)
    return even, odd


def lane_cumsum(x):
    width = x.shape[1]
    lane = lax.broadcasted_iota(jnp.int32, x.shape, 1)
    step = 1
    while step < width:
        x = x + jnp.where(lane >= step, pltpu.roll(x, step, 1), 0)
        step *= 2
    return x


def lookup(table_ref, index):
    value = jnp.zeros(index.shape, F32)
    for part in range(table_ref.shape[0]):
        row = jnp.broadcast_to(table_ref[part : part + 1, :], index.shape)
        near = jnp.clip(index - 128 * part, 0, 127)
        found = jnp.take_along_axis(row, near, axis=1)
        value = jnp.where(index // 128 == part, found, value)
    return value


def prep_kernel(
    me_ref, map_ref, val_ref, screen_ref, ci_ref, vi_ref, ce_ref, ve_ref, sent_ref, place_ref, gap_ref
):
    n, rows = map_ref.shape
    per_peer = rows // n
    me = me_ref[0]
    gap_ref[...] = lookup(ce_ref, ci_ref[...]) - lookup(ve_ref, vi_ref[...])
    scaled = (val_ref[...].astype(F32) * screen_ref[...]).astype(BF16)
    block = lax.broadcasted_iota(jnp.int32, (n, rows), 0)
    own = jnp.broadcast_to(map_ref[pl.ds(me, 1), :], (n, rows))
    goes = (own >= block * rows) & (own < (block + 1) * rows)
    rank = lane_cumsum(goes.astype(jnp.int32)) - 1
    position = jnp.sum(jnp.where(goes, rank + block * per_peer, 0), axis=0, keepdims=True)
    chunk = 128
    for c in range(rows // chunk):
        ids = lax.broadcasted_iota(jnp.int32, (chunk, rows), 0) + c * chunk
        pick = jnp.where(ids == position, 1.0, 0.0).astype(BF16)
        sent_ref[c * chunk : (c + 1) * chunk, :] = jnp.dot(
            pick, scaled, preferred_element_type=F32
        ).astype(BF16)
    slots = map_ref[...] - me * rows
    lands = (slots >= 0) & (slots < rows)
    arrival = jnp.where(lands, lane_cumsum(lands.astype(jnp.int32)) - 1, -1)
    slots = slots.astype(F32)
    ids = lax.broadcasted_iota(jnp.int32, (per_peer, rows), 0)
    lane = lax.broadcasted_iota(jnp.int32, (per_peer, rows), 1).astype(F32)
    for q in range(n):
        hit = ids == arrival[q : q + 1, :]
        slot = jnp.sum(jnp.where(hit, slots[q : q + 1, :], 0.0), axis=1, keepdims=True)
        place_ref[q * per_peer : (q + 1) * per_peer, :] = jnp.where(slot == lane, 1.0, 0.0).astype(BF16)


def tile_kernel(me_ref, val_ref, screen_ref, a_ref, b_ref, out_ref, scaled_ref):
    del me_ref

    @pl.when(pl.program_id(0) == 0)
    def _():
        scaled_ref[...] = (val_ref[...].astype(F32) * screen_ref[...]).astype(BF16)

    cond = jnp.concatenate([a_ref[0], b_ref[0]], axis=0)
    out_ref[0] = lax.dot_general(
        scaled_ref[...], cond, (((1,), (1,)), ((), ())), preferred_element_type=F32
    ).astype(BF16)


def final_kernel(arrived_ref, place_ref, gap_ref, trial_ref, out_ref):
    rows = trial_ref.shape[1]
    moved = jnp.dot(arrived_ref[...], place_ref[...], preferred_element_type=F32)
    for c in range(rows // 128):
        part = slice(c * 128, (c + 1) * 128)
        out_ref[:, part] = (
            gap_ref[c : c + 1, :] * trial_ref[:, part].astype(F32) + moved[:, part]
        ).astype(BF16)


def per_device(
    mat_val,
    mat_cond,
    screening,
    trial_cols,
    trial_rows,
    row_map,
    val_index,
    cond_index,
    val_energy,
    cond_energy,
):
    n = lax.axis_size("pairs")
    m = lax.axis_size("rep")
    rows, depth = mat_val.shape
    cols = mat_cond.shape[0]
    vecs = trial_cols.shape[1]
    per_peer = rows // n
    me = lax.axis_index("pairs").astype(jnp.int32).reshape(1)
    screen = screening.reshape(1, depth)

    trial = trial_cols.T
    wide = jnp.concatenate([trial] + [exchange(trial, "rep", k) for k in range(1, m)], axis=0)
    cond_even, cond_odd = pair_gather(mat_cond)
    cond_all = jnp.stack([cond_even, cond_odd], axis=1).reshape(n, cols, depth)
    vec_even, vec_odd = pair_gather(wide)
    vec_all = jnp.stack([vec_even, vec_odd], axis=1).reshape(n, m * vecs, cols)
    vec_all = vec_all.transpose(1, 0, 2).reshape(m * vecs, n * cols)

    sent, place, gap = pl.pallas_call(
        prep_kernel,
        grid_spec=pltpu.PrefetchScalarGridSpec(
            num_scalar_prefetch=1,
            grid=(1,),
            in_specs=[pl.BlockSpec(s, lambda i, _: (0, 0)) for s in (
                (n, rows), (rows, depth), (1, depth), (rows // 128, 128), (rows // 128, 128),
                (cond_energy.shape[0] // 128, 128), (val_energy.shape[0] // 128, 128))],
            out_specs=[pl.BlockSpec(s, lambda i, _: (0, 0)) for s in (
                (rows, depth), (rows, rows), (rows // 128, 128))],
        ),
        out_shape=(
            jax.ShapeDtypeStruct((rows, depth), BF16),
            jax.ShapeDtypeStruct((rows, rows), BF16),
            jax.ShapeDtypeStruct((rows // 128, 128), F32),
        ),
        cost_estimate=pl.CostEstimate(
            flops=2 * rows * rows * depth, bytes_accessed=6 * rows * depth, transcendentals=0),
        name="prep",
    )(
        me,
        row_map.reshape(n, rows),
        mat_val,
        screen,
        cond_index.reshape(-1, 128),
        val_index.reshape(-1, 128),
        cond_energy.reshape(-1, 128),
        val_energy.reshape(-1, 128),
    )

    mixed = jnp.dot(
        vec_all, cond_all.reshape(n * cols, depth), preferred_element_type=F32
    ).astype(BF16)
    partial = lax.dot_general(mixed, sent, (((1,), (1,)), ((), ())), preferred_element_type=F32)
    part = [partial[k * vecs : (k + 1) * vecs] for k in range(m)]
    step = m // 2
    while step >= 1:
        arrived = {}
        bit = m // 2 // step
        for k in sorted((k for k in range(len(part)) if part[k] is not None and k & bit), reverse=True):
            arrived[k ^ bit] = exchange(part[k].astype(BF16), "rep", bit)
            part[k] = None
        for k, value in arrived.items():
            part[k] = part[k] + value.astype(F32)
        step //= 2
    total = part[0].astype(BF16)

    shipped = lax.all_to_all(
        total.reshape(vecs, n, per_peer).transpose(1, 0, 2), "pairs", split_axis=0, concat_axis=0, tiled=True
    )
    shipped = shipped.transpose(1, 0, 2).reshape(vecs, rows)

    tiles = pl.pallas_call(
        tile_kernel,
        grid_spec=pltpu.PrefetchScalarGridSpec(
            num_scalar_prefetch=1,
            grid=(n // 2,),
            in_specs=[
                pl.BlockSpec((rows, depth), lambda d, me: (0, 0)),
                pl.BlockSpec((1, depth), lambda d, me: (0, 0)),
                pl.BlockSpec((1, cols, depth), lambda d, me: ((2 * d) ^ me[0], 0, 0)),
                pl.BlockSpec((1, cols, depth), lambda d, me: ((2 * d + 1) ^ me[0], 0, 0)),
            ],
            out_specs=pl.BlockSpec((1, rows, 2 * cols), lambda d, me: (0, 0, d)),
            scratch_shapes=[pltpu.VMEM((rows, depth), BF16)],
        ),
        out_shape=jax.ShapeDtypeStruct((1, rows, n * cols), BF16),
        cost_estimate=pl.CostEstimate(
            flops=2 * rows * depth * n * cols, bytes_accessed=2 * rows * (depth + n * cols), transcendentals=0),
        name="tiles",
    )(me, mat_val, screen, cond_all, cond_all)

    response = pl.pallas_call(
        final_kernel,
        out_shape=jax.ShapeDtypeStruct((vecs, rows), BF16),
        cost_estimate=pl.CostEstimate(
            flops=2 * rows * rows * vecs, bytes_accessed=2 * rows * rows, transcendentals=0),
        name="final",
    )(shipped, place, gap, trial_rows.T)
    return (response.T, tiles)


def solution(mesh):
    in_specs = (
        P("pairs", "rep"),
        P("pairs", "rep"),
        P("rep"),
        P("pairs", "rep"),
        P("pairs", "rep"),
        P(),
        P("pairs"),
        P("pairs"),
        P(),
        P(),
    )
    out_specs = (P("pairs", "rep"), P("rep", "pairs", None))
    return jax.shard_map(
        per_device, mesh=mesh, in_specs=in_specs, out_specs=out_specs, check_vma=False
    )
```

```python
import jax
import jax.numpy as jnp
from jax import lax
from jax.experimental import pallas as pl
from jax.experimental.pallas import tpu as pltpu
from jax.sharding import PartitionSpec as P

F32 = jnp.float32
BF16 = jnp.bfloat16
SCALAR = pl.BlockSpec(memory_space=pltpu.SMEM)
WHOLE = pl.BlockSpec(memory_space=pltpu.VMEM)


def roomy(mib):
    return pltpu.CompilerParams(vmem_limit_bytes=mib << 20)


def exchange(x, axis, mask):
    size = lax.axis_size(axis)
    return lax.ppermute(x, axis, [(i, i ^ mask) for i in range(size)])


def split_exchange(x, even_mask, odd_mask):
    size = lax.axis_size("pairs")
    return lax.ppermute(x, "pairs", [(i, i ^ (odd_mask if i & 1 else even_mask)) for i in range(size)])


def in_order(odd, own, partner):
    return jnp.where(odd, jnp.stack([partner, own]), jnp.stack([own, partner]))


def lane_cumsum(x):
    width = x.shape[1]
    lane = lax.broadcasted_iota(jnp.int32, x.shape, 1)
    step = 1
    while step < width:
        x = x + jnp.where(lane >= step, pltpu.roll(x, step, 1), 0)
        step *= 2
    return x


def lookup(table_ref, index):
    value = jnp.zeros(index.shape, F32)
    for part in range(table_ref.shape[0]):
        row = jnp.broadcast_to(table_ref[part : part + 1, :], index.shape)
        near = jnp.clip(index - 128 * part, 0, 127)
        found = jnp.take_along_axis(row, near, axis=1)
        value = jnp.where(index // 128 == part, found, value)
    return value


def load_kernel(n, me_ref, map_hbm, val_hbm, screen_hbm, scaled_ref, order_ref, map_ref, val_ref, screen_ref, sems):
    rows = val_ref.shape[0]
    per_peer = rows // n
    lanes = rows // 128
    tall = rows // 4
    first = pl.multiple_of(me_ref[0] * lanes, lanes)
    head = [
        pltpu.make_async_copy(screen_hbm, screen_ref, sems.at[0]),
        pltpu.make_async_copy(map_hbm.at[pl.ds(first, lanes), :], map_ref, sems.at[1]),
    ]
    body = [
        pltpu.make_async_copy(
            val_hbm.at[pl.ds(k * tall, tall), :], val_ref.at[pl.ds(k * tall, tall), :], sems.at[2 + k])
        for k in range(4)
    ]
    for copy in head + body:
        copy.start()
    for copy in head:
        copy.wait()
    own = jnp.concatenate([map_ref[c : c + 1, :] for c in range(lanes)], axis=1)
    own = jnp.broadcast_to(own, (n, rows))
    block = lax.broadcasted_iota(jnp.int32, (n, rows), 0)
    goes = (own >= block * rows) & (own < (block + 1) * rows)
    rank = lane_cumsum(goes.astype(jnp.int32)) - 1
    order_ref[...] = jnp.sum(jnp.where(goes, rank + block * per_peer, 0), axis=0, keepdims=True)
    for k, copy in enumerate(body):
        copy.wait()
        part = slice(k * tall, (k + 1) * tall)
        scaled_ref[part, :] = (val_ref[part, :].astype(F32) * screen_ref[...]).astype(BF16)


def sent_kernel(first, order_ref, scaled_ref, sent_ref):
    rows = scaled_ref.shape[0]
    chunk = 128
    for c in range(sent_ref.shape[0] // chunk):
        ids = lax.broadcasted_iota(jnp.int32, (chunk, rows), 0) + (first + c * chunk)
        pick = jnp.where(ids == order_ref[...], 1.0, 0.0).astype(BF16)
        sent_ref[c * chunk : (c + 1) * chunk, :] = jnp.dot(
            pick, scaled_ref[...], preferred_element_type=F32
        ).astype(BF16)


def place_kernel(n, rows, me_ref, map_ref, ci_ref, vi_ref, ce_ref, ve_ref, place_ref, gap_ref):
    per_peer = rows // n
    lanes = rows // 128
    gap_ref[...] = lookup(ce_ref, ci_ref[...]) - lookup(ve_ref, vi_ref[...])
    grid = jnp.concatenate([map_ref[pl.ds(c, n, stride=lanes), :] for c in range(lanes)], axis=1)
    slots = grid - me_ref[0] * rows
    lands = (slots >= 0) & (slots < rows)
    arrival = jnp.where(lands, lane_cumsum(lands.astype(jnp.int32)) - 1, -1)
    slots = slots.astype(F32)
    ids = lax.broadcasted_iota(jnp.int32, (per_peer, rows), 0)
    lane = lax.broadcasted_iota(jnp.int32, (per_peer, rows), 1).astype(F32)
    for q in range(n):
        hit = ids == arrival[q : q + 1, :]
        slot = jnp.sum(jnp.where(hit, slots[q : q + 1, :], 0.0), axis=1, keepdims=True)
        place_ref[q * per_peer : (q + 1) * per_peer, :] = jnp.where(slot == lane, 1.0, 0.0).astype(BF16)


def tile_kernel(me_ref, scaled_ref, cond_ref, out_ref):
    chips, _, cols, depth = cond_ref.shape
    chip = me_ref[0] // 2
    for k in range(chips):
        tile = lax.dot_general(
            scaled_ref[...],
            cond_ref[k].reshape(2 * cols, depth),
            (((1,), (1,)), ((), ())),
            preferred_element_type=F32,
        )
        start = pl.multiple_of((chip ^ k) * (2 * cols), 128)
        out_ref[0, :, pl.ds(start, 2 * cols)] = tile.astype(BF16)


def apply_kernel(m, n, me_ref, mixed_ref, *refs):
    shares = (len(refs) - 1) // 2
    out_ref = refs[-1]
    half, width = out_ref.shape[1:]
    per_peer = width // 2
    odd = (me_ref[0] & 1) == 1
    for share in range(shares):
        own, other = (
            lax.dot_general(
                mixed_ref[...], ref[...], (((1,), (1,)), ((), ())), preferred_element_type=F32
            ).astype(BF16)
            for ref in (refs[share], refs[shares + share])
        )
        first, second = jnp.where(odd, other, own), jnp.where(odd, own, other)
        for d in range(n // shares):
            part = slice(d * per_peer, (d + 1) * per_peer)
            for k in range(m):
                to = ((share * n) // shares + d) * m + k
                out_ref[to, :, :per_peer] = first[k * half : (k + 1) * half, part]
                out_ref[to, :, per_peer:] = second[k * half : (k + 1) * half, part]


def final_kernel(n, m, arrived_ref, place_ref, gap_ref, trial_ref, out_ref, row_ref):
    width = out_ref.shape[1]
    half, pair = arrived_ref.shape[1:]
    for q in range(n):
        total = arrived_ref[q * m].astype(F32)
        for k in range(1, m):
            total = total + arrived_ref[q * m + k].astype(F32)
        at = (q & 1) * half
        row_ref[at : at + half, (q // 2) * pair : (q // 2 + 1) * pair] = total.astype(BF16)
    moved = jnp.dot(row_ref[...], place_ref[...], preferred_element_type=F32)
    for c in range(width // 128):
        part = slice(c * 128, (c + 1) * 128)
        gap = gap_ref[c : c + 1, :]
        out_ref[:, part] = (gap * trial_ref[:, part].astype(F32) + moved[:, part]).astype(BF16)


def cond_gather(both, odd):
    n = lax.axis_size("pairs")
    if n != 8:
        every = both[None]
        mask = 2
        while mask < n:
            every = jnp.concatenate([every, exchange(every, "pairs", mask)])
            mask *= 2
        return every
    far = split_exchange(both, 2, 4)
    corner = split_exchange(jnp.where(odd, far[1], far[0]), 4, 2)
    mine = jnp.concatenate([far, corner[None]])
    other = exchange(mine, "pairs", 1)
    first, second = jnp.where(odd, other, mine), jnp.where(odd, mine, other)
    return jnp.stack([both, first[:2], second[:2], jnp.stack([first[2], second[2]])])


def per_device(
    mat_val,
    mat_cond,
    screening,
    trial_cols,
    trial_rows,
    row_map,
    val_index,
    cond_index,
    val_energy,
    cond_energy,
):
    n = lax.axis_size("pairs")
    m = lax.axis_size("rep")
    rows, depth = mat_val.shape
    cols = mat_cond.shape[0]
    vecs = trial_cols.shape[1]
    half = vecs // 2
    per_peer = rows // n
    own = lax.axis_index("pairs").astype(jnp.int32)
    layer = lax.axis_index("rep").astype(jnp.int32)
    odd = (own & 1) == 1
    me = own.reshape(1)
    screen = screening.reshape(1, depth)
    map_lanes = row_map.reshape(-1, 128)

    trial = trial_cols.T
    low, high = trial[:half], trial[half:]
    got = exchange(jnp.where(odd, low, high), "pairs", 1)
    vec = in_order(odd, jnp.where(odd, high, low), got)
    vec = vec.transpose(1, 0, 2).reshape(half, 2 * cols)
    turns = [vec]
    for k in range(1, m):
        turns.append(lax.ppermute(vec, "rep", [(i, (i + k) % m) for i in range(m)]))
    vec_all = []
    for k in range(m):
        block = turns[0]
        for t in range(1, m):
            block = jnp.where(lax.rem(layer - t + m, m) == k, turns[t], block)
        vec_all.append(block)
    vec_all = jnp.concatenate(vec_all)

    both = in_order(odd, mat_cond, exchange(mat_cond, "pairs", 1))

    shares = 2
    far_away = pl.BlockSpec(memory_space=pltpu.HBM)
    scaled, order = pl.pallas_call(
        lambda *refs: load_kernel(n, *refs),
        in_specs=[SCALAR, far_away, far_away, far_away],
        out_specs=(WHOLE, WHOLE),
        out_shape=(
            jax.ShapeDtypeStruct((rows, depth), BF16),
            jax.ShapeDtypeStruct((1, rows), jnp.int32),
        ),
        scratch_shapes=[
            pltpu.VMEM((rows // 128, 128), jnp.int32),
            pltpu.VMEM((rows, depth), BF16),
            pltpu.VMEM((1, depth), F32),
            pltpu.SemaphoreType.DMA((6,)),
        ],
        cost_estimate=pl.CostEstimate(flops=rows * depth, bytes_accessed=4 * rows * depth, transcendentals=0),
        compiler_params=roomy(12),
        name="load",
    )(me, *(pltpu.with_memory_space_constraint(x, pltpu.HBM) for x in (map_lanes, mat_val, screen)))
    shares = 1
    sent = [pl.pallas_call(
        lambda *refs, share=share: sent_kernel(share * (rows // shares), *refs),
        in_specs=[WHOLE, WHOLE],
        out_specs=WHOLE,
        out_shape=jax.ShapeDtypeStruct((rows // shares, depth), BF16),
        cost_estimate=pl.CostEstimate(
            flops=2 * rows * rows * depth // shares, bytes_accessed=4 * rows * depth, transcendentals=0),
        compiler_params=roomy(12),
    )(order, scaled) for share in range(shares)]
    sent_other = [exchange(part, "pairs", 1) for part in sent]

    mixed = jnp.dot(vec_all, both.reshape(2 * cols, depth), preferred_element_type=F32)
    masks = [2**b for b in range(1, n.bit_length() - 1)]
    for even_mask, odd_mask in zip(masks, masks[::-1]):
        mixed = mixed + split_exchange(mixed.astype(BF16), even_mask, odd_mask).astype(F32)
    mixed = mixed.astype(BF16)
    if per_peer % 128 == 0:
        outgoing = pl.pallas_call(
            lambda *refs: apply_kernel(m, n, *refs),
            in_specs=[SCALAR] + [WHOLE] * (1 + 2 * shares),
            out_specs=WHOLE,
            compiler_params=roomy(12),
            out_shape=jax.ShapeDtypeStruct((n * m, half, 2 * per_peer), BF16),
            cost_estimate=pl.CostEstimate(
                flops=4 * rows * depth * m * half, bytes_accessed=4 * rows * depth, transcendentals=0),
            name="apply",
        )(me, mixed, *sent, *sent_other)
    else:
        rows_both = in_order(odd, jnp.concatenate(sent), jnp.concatenate(sent_other))
        rows_both = rows_both.reshape(2, n, per_peer, depth).transpose(1, 0, 2, 3).reshape(2 * rows, depth)
        partial = lax.dot_general(
            mixed, rows_both, (((1,), (1,)), ((), ())), preferred_element_type=F32
        ).astype(BF16)
        outgoing = partial.reshape(m, half, n, 2 * per_peer).transpose(2, 0, 1, 3)
        outgoing = outgoing.reshape(n * m, half, 2 * per_peer)
    arrived = lax.all_to_all(outgoing, ("pairs", "rep"), split_axis=0, concat_axis=0, tiled=True)

    cond_all = cond_gather(both, odd)
    tall = min(rows, 256)
    tiles = pl.pallas_call(
        tile_kernel,
        grid_spec=pltpu.PrefetchScalarGridSpec(
            num_scalar_prefetch=1,
            grid=(rows // tall,),
            in_specs=[
                pl.BlockSpec((tall, depth), lambda d, me: (d, 0)),
                pl.BlockSpec((n // 2, 2, cols, depth), lambda d, me: (0, 0, 0, 0)),
            ],
            out_specs=pl.BlockSpec((1, tall, n * cols), lambda d, me: (0, d, 0)),
        ),
        out_shape=jax.ShapeDtypeStruct((1, rows, n * cols), BF16),
        cost_estimate=pl.CostEstimate(
            flops=2 * rows * depth * n * cols, bytes_accessed=2 * rows * (depth + n * cols), transcendentals=0),
        compiler_params=roomy(16),
        name="tiles",
    )(me, scaled, cond_all)

    place, gap = pl.pallas_call(
        lambda *refs: place_kernel(n, rows, *refs),
        in_specs=[SCALAR] + [WHOLE] * 5,
        out_specs=(WHOLE, WHOLE),
        out_shape=(
            jax.ShapeDtypeStruct((rows, rows), BF16),
            jax.ShapeDtypeStruct((rows // 128, 128), F32),
        ),
        cost_estimate=pl.CostEstimate(
            flops=8 * rows * rows, bytes_accessed=2 * rows * rows, transcendentals=0),
        compiler_params=roomy(12),
        name="place",
    )(
        me,
        map_lanes,
        cond_index.reshape(-1, 128),
        val_index.reshape(-1, 128),
        cond_energy.reshape(-1, 128),
        val_energy.reshape(-1, 128),
    )

    if per_peer % 128 != 0:
        arrived = jnp.sum(arrived.reshape(n // 2, 2, m, half, 2 * per_peer).astype(F32), axis=2).astype(BF16)
        arrived = arrived.transpose(1, 2, 0, 3).reshape(2, half, rows)
    parts, layers = (n, m) if per_peer % 128 == 0 else (2, 1)
    response = pl.pallas_call(
        lambda *refs: final_kernel(parts, layers, *refs),
        in_specs=[WHOLE] * 4,
        out_specs=WHOLE,
        compiler_params=roomy(12),
        out_shape=jax.ShapeDtypeStruct((vecs, rows), BF16),
        scratch_shapes=[pltpu.VMEM((vecs, rows), BF16)],
        cost_estimate=pl.CostEstimate(
            flops=2 * rows * rows * vecs, bytes_accessed=2 * rows * rows, transcendentals=0),
        name="final",
    )(arrived, place, gap, trial_rows.T)
    return (response.T, tiles)


def solution(mesh):
    in_specs = (
        P("pairs", "rep"),
        P("pairs", "rep"),
        P("rep"),
        P("pairs", "rep"),
        P("pairs", "rep"),
        P(),
        P("pairs"),
        P("pairs"),
        P(),
        P(),
    )
    out_specs = (P("pairs", "rep"), P("rep", "pairs", None))

    return jax.shard_map(per_device, mesh=mesh, in_specs=in_specs, out_specs=out_specs, check_vma=False)
```

```python
import jax
import jax.numpy as jnp
from jax import lax
from jax.experimental import pallas as pl
from jax.experimental.pallas import tpu as pltpu
from jax.sharding import PartitionSpec as P

F32 = jnp.float32
BF16 = jnp.bfloat16
SCALAR = pl.BlockSpec(memory_space=pltpu.SMEM)
WHOLE = pl.BlockSpec(memory_space=pltpu.VMEM)


def roomy(mib):
    return pltpu.CompilerParams(vmem_limit_bytes=mib << 20)


def exchange(x, axis, mask):
    size = lax.axis_size(axis)
    return lax.ppermute(x, axis, [(i, i ^ mask) for i in range(size)])


def split_exchange(x, even_mask, odd_mask):
    size = lax.axis_size("pairs")
    return lax.ppermute(x, "pairs", [(i, i ^ (odd_mask if i & 1 else even_mask)) for i in range(size)])


def in_order(odd, own, partner):
    return jnp.where(odd, jnp.stack([partner, own]), jnp.stack([own, partner]))


def lane_cumsum(x):
    width = x.shape[1]
    lane = lax.broadcasted_iota(jnp.int32, x.shape, 1)
    step = 1
    while step < width:
        x = x + jnp.where(lane >= step, pltpu.roll(x, step, 1), 0)
        step *= 2
    return x


def lookup(table_ref, index):
    value = jnp.zeros(index.shape, F32)
    for part in range(table_ref.shape[0]):
        row = jnp.broadcast_to(table_ref[part : part + 1, :], index.shape)
        near = jnp.clip(index - 128 * part, 0, 127)
        found = jnp.take_along_axis(row, near, axis=1)
        value = jnp.where(index // 128 == part, found, value)
    return value


def load_kernel(
    n, me_ref, map_hbm, val_hbm, screen_hbm, cond_hbm, trial_hbm,
    scaled_ref, order_ref, cond_ref, trial_ref, map_ref, val_ref, screen_ref, sems,
):
    rows = val_ref.shape[0]
    per_peer = rows // n
    lanes = rows // 128
    tall = rows // 4
    first = pl.multiple_of(me_ref[0] * lanes, lanes)
    head = [
        pltpu.make_async_copy(screen_hbm, screen_ref, sems.at[0]),
        pltpu.make_async_copy(map_hbm.at[pl.ds(first, lanes), :], map_ref, sems.at[1]),
    ]
    tail = [
        pltpu.make_async_copy(cond_hbm, cond_ref, sems.at[6]),
        pltpu.make_async_copy(trial_hbm, trial_ref, sems.at[7]),
    ]
    body = [
        pltpu.make_async_copy(
            val_hbm.at[pl.ds(k * tall, tall), :], val_ref.at[pl.ds(k * tall, tall), :], sems.at[2 + k])
        for k in range(4)
    ]
    for copy in head + body + tail:
        copy.start()
    for copy in head:
        copy.wait()
    own = jnp.concatenate([map_ref[c : c + 1, :] for c in range(lanes)], axis=1)
    own = jnp.broadcast_to(own, (n, rows))
    block = lax.broadcasted_iota(jnp.int32, (n, rows), 0)
    goes = (own >= block * rows) & (own < (block + 1) * rows)
    rank = lane_cumsum(goes.astype(jnp.int32)) - 1
    order_ref[...] = jnp.sum(jnp.where(goes, rank + block * per_peer, 0), axis=0, keepdims=True)
    for k, copy in enumerate(body):
        copy.wait()
        part = slice(k * tall, (k + 1) * tall)
        scaled_ref[part, :] = (val_ref[part, :].astype(F32) * screen_ref[...]).astype(BF16)
    for copy in tail:
        copy.wait()


def sent_kernel(first, order_ref, scaled_ref, sent_ref):
    rows = scaled_ref.shape[0]
    chunk = 128
    for c in range(sent_ref.shape[0] // chunk):
        ids = lax.broadcasted_iota(jnp.int32, (chunk, rows), 0) + (first + c * chunk)
        pick = jnp.where(ids == order_ref[...], 1.0, 0.0).astype(BF16)
        sent_ref[c * chunk : (c + 1) * chunk, :] = jnp.dot(
            pick, scaled_ref[...], preferred_element_type=F32
        ).astype(BF16)


def place_kernel(n, rows, me_ref, map_ref, ci_ref, vi_ref, ce_ref, ve_ref, place_ref, gap_ref):
    per_peer = rows // n
    lanes = rows // 128
    gap_ref[...] = lookup(ce_ref, ci_ref[...]) - lookup(ve_ref, vi_ref[...])
    grid = jnp.concatenate([map_ref[pl.ds(c, n, stride=lanes), :] for c in range(lanes)], axis=1)
    slots = grid - me_ref[0] * rows
    lands = (slots >= 0) & (slots < rows)
    arrival = jnp.where(lands, lane_cumsum(lands.astype(jnp.int32)) - 1, -1)
    slots = slots.astype(F32)
    ids = lax.broadcasted_iota(jnp.int32, (per_peer, rows), 0)
    lane = lax.broadcasted_iota(jnp.int32, (per_peer, rows), 1).astype(F32)
    for q in range(n):
        hit = ids == arrival[q : q + 1, :]
        slot = jnp.sum(jnp.where(hit, slots[q : q + 1, :], 0.0), axis=1, keepdims=True)
        place_ref[q * per_peer : (q + 1) * per_peer, :] = jnp.where(slot == lane, 1.0, 0.0).astype(BF16)


def tile_kernel(me_ref, scaled_ref, cond_ref, out_ref):
    chips, _, cols, depth = cond_ref.shape
    chip = me_ref[0] // 2
    for k in range(chips):
        tile = lax.dot_general(
            scaled_ref[...],
            cond_ref[k].reshape(2 * cols, depth),
            (((1,), (1,)), ((), ())),
            preferred_element_type=F32,
        )
        start = pl.multiple_of((chip ^ k) * (2 * cols), 128)
        out_ref[0, :, pl.ds(start, 2 * cols)] = tile.astype(BF16)


def apply_kernel(m, n, me_ref, mixed_ref, *refs):
    shares = (len(refs) - 1) // 2
    out_ref = refs[-1]
    half, width = out_ref.shape[1:]
    per_peer = width // 2
    odd = (me_ref[0] & 1) == 1
    for share in range(shares):
        own, other = (
            lax.dot_general(
                mixed_ref[...], ref[...], (((1,), (1,)), ((), ())), preferred_element_type=F32
            ).astype(BF16)
            for ref in (refs[share], refs[shares + share])
        )
        first, second = jnp.where(odd, other, own), jnp.where(odd, own, other)
        for d in range(n // shares):
            part = slice(d * per_peer, (d + 1) * per_peer)
            for k in range(m):
                to = ((share * n) // shares + d) * m + k
                out_ref[to, :, :per_peer] = first[k * half : (k + 1) * half, part]
                out_ref[to, :, per_peer:] = second[k * half : (k + 1) * half, part]


def final_kernel(n, m, arrived_ref, place_ref, gap_ref, trial_ref, out_ref, row_ref):
    width = out_ref.shape[1]
    half, pair = arrived_ref.shape[1:]
    for q in range(n):
        total = arrived_ref[q * m].astype(F32)
        for k in range(1, m):
            total = total + arrived_ref[q * m + k].astype(F32)
        at = (q & 1) * half
        row_ref[at : at + half, (q // 2) * pair : (q // 2 + 1) * pair] = total.astype(BF16)
    moved = jnp.dot(row_ref[...], place_ref[...], preferred_element_type=F32)
    for c in range(width // 128):
        part = slice(c * 128, (c + 1) * 128)
        gap = gap_ref[c : c + 1, :]
        out_ref[:, part] = (gap * trial_ref[:, part].astype(F32) + moved[:, part]).astype(BF16)


def cond_gather(both, odd):
    n = lax.axis_size("pairs")
    if n != 8:
        every = both[None]
        mask = 2
        while mask < n:
            every = jnp.concatenate([every, exchange(every, "pairs", mask)])
            mask *= 2
        return every
    far = split_exchange(both, 2, 4)
    corner = split_exchange(jnp.where(odd, far[1], far[0]), 4, 2)
    mine = jnp.concatenate([far, corner[None]])
    other = exchange(mine, "pairs", 1)
    first, second = jnp.where(odd, other, mine), jnp.where(odd, mine, other)
    return jnp.stack([both, first[:2], second[:2], jnp.stack([first[2], second[2]])])


def per_device(
    mat_val,
    mat_cond,
    screening,
    trial_cols,
    trial_rows,
    row_map,
    val_index,
    cond_index,
    val_energy,
    cond_energy,
):
    n = lax.axis_size("pairs")
    m = lax.axis_size("rep")
    rows, depth = mat_val.shape
    cols = mat_cond.shape[0]
    vecs = trial_cols.shape[1]
    half = vecs // 2
    per_peer = rows // n
    own = lax.axis_index("pairs").astype(jnp.int32)
    layer = lax.axis_index("rep").astype(jnp.int32)
    odd = (own & 1) == 1
    me = own.reshape(1)
    screen = screening.reshape(1, depth)
    map_lanes = row_map.reshape(-1, 128)

    turns = [None]
    for k in range(1, m):
        turns.append(lax.ppermute(trial_cols.T, "rep", [(i, (i + k) % m) for i in range(m)]))
    cond_other = exchange(mat_cond, "pairs", 1)

    shares = 2
    far_away = pl.BlockSpec(memory_space=pltpu.HBM)
    scaled, order, cond_own, turns[0] = pl.pallas_call(
        lambda *refs: load_kernel(n, *refs),
        in_specs=[SCALAR] + [far_away] * 5,
        out_specs=(WHOLE,) * 4,
        out_shape=(
            jax.ShapeDtypeStruct((rows, depth), BF16),
            jax.ShapeDtypeStruct((1, rows), jnp.int32),
            jax.ShapeDtypeStruct((cols, depth), BF16),
            jax.ShapeDtypeStruct((vecs, cols), BF16),
        ),
        scratch_shapes=[
            pltpu.VMEM((rows // 128, 128), jnp.int32),
            pltpu.VMEM((rows, depth), BF16),
            pltpu.VMEM((1, depth), F32),
            pltpu.SemaphoreType.DMA((8,)),
        ],
        cost_estimate=pl.CostEstimate(flops=rows * depth, bytes_accessed=4 * rows * depth, transcendentals=0),
        compiler_params=roomy(8),
        name="load",
    )(me, *(pltpu.with_memory_space_constraint(x, pltpu.HBM) for x in (map_lanes, mat_val, screen, mat_cond, trial_cols.T)))
    both = in_order(odd, cond_own, cond_other)
    wide = []
    for k in range(m):
        block = turns[0]
        for t in range(1, m):
            block = jnp.where(lax.rem(layer - t + m, m) == k, turns[t], block)
        wide.append(block)
    wide = jnp.stack(wide)
    low, high = wide[:, :half], wide[:, half:]
    got = exchange(jnp.where(odd, low, high), "pairs", 1)
    kept = jnp.where(odd, high, low)
    vec_all = jnp.where(odd, jnp.concatenate([got, kept], axis=2), jnp.concatenate([kept, got], axis=2))
    vec_all = vec_all.reshape(m * half, 2 * cols)
    shares = 1
    sent = [pl.pallas_call(
        lambda *refs, share=share: sent_kernel(share * (rows // shares), *refs),
        in_specs=[WHOLE, WHOLE],
        out_specs=WHOLE,
        out_shape=jax.ShapeDtypeStruct((rows // shares, depth), BF16),
        cost_estimate=pl.CostEstimate(
            flops=2 * rows * rows * depth // shares, bytes_accessed=4 * rows * depth, transcendentals=0),
        compiler_params=roomy(8),
    )(order, scaled) for share in range(shares)]
    sent_other = [exchange(part, "pairs", 1) for part in sent]

    mixed = jnp.dot(vec_all, both.reshape(2 * cols, depth), preferred_element_type=F32)
    masks = [2**b for b in range(1, n.bit_length() - 1)]
    for even_mask, odd_mask in zip(masks, masks[::-1]):
        mixed = mixed + split_exchange(mixed.astype(BF16), even_mask, odd_mask).astype(F32)
    mixed = mixed.astype(BF16)
    if per_peer % 128 == 0:
        outgoing = pl.pallas_call(
            lambda *refs: apply_kernel(m, n, *refs),
            in_specs=[SCALAR] + [WHOLE] * (1 + 2 * shares),
            out_specs=WHOLE,
            compiler_params=roomy(8),
            out_shape=jax.ShapeDtypeStruct((n * m, half, 2 * per_peer), BF16),
            cost_estimate=pl.CostEstimate(
                flops=4 * rows * depth * m * half, bytes_accessed=4 * rows * depth, transcendentals=0),
            name="apply",
        )(me, mixed, *sent, *sent_other)
    else:
        rows_both = in_order(odd, jnp.concatenate(sent), jnp.concatenate(sent_other))
        rows_both = rows_both.reshape(2, n, per_peer, depth).transpose(1, 0, 2, 3).reshape(2 * rows, depth)
        partial = lax.dot_general(
            mixed, rows_both, (((1,), (1,)), ((), ())), preferred_element_type=F32
        ).astype(BF16)
        outgoing = partial.reshape(m, half, n, 2 * per_peer).transpose(2, 0, 1, 3)
        outgoing = outgoing.reshape(n * m, half, 2 * per_peer)
    arrived = lax.all_to_all(outgoing, ("pairs", "rep"), split_axis=0, concat_axis=0, tiled=True)

    cond_all = cond_gather(both, odd)
    tall = min(rows, 256)
    tiles = pl.pallas_call(
        tile_kernel,
        grid_spec=pltpu.PrefetchScalarGridSpec(
            num_scalar_prefetch=1,
            grid=(rows // tall,),
            in_specs=[
                pl.BlockSpec((tall, depth), lambda d, me: (d, 0)),
                pl.BlockSpec((n // 2, 2, cols, depth), lambda d, me: (0, 0, 0, 0)),
            ],
            out_specs=pl.BlockSpec((1, tall, n * cols), lambda d, me: (0, d, 0)),
        ),
        out_shape=jax.ShapeDtypeStruct((1, rows, n * cols), BF16),
        cost_estimate=pl.CostEstimate(
            flops=2 * rows * depth * n * cols, bytes_accessed=2 * rows * (depth + n * cols), transcendentals=0),
        compiler_params=roomy(8),
        name="tiles",
    )(me, scaled, cond_all)

    place, gap = pl.pallas_call(
        lambda *refs: place_kernel(n, rows, *refs),
        in_specs=[SCALAR] + [WHOLE] * 5,
        out_specs=(WHOLE, WHOLE),
        out_shape=(
            jax.ShapeDtypeStruct((rows, rows), BF16),
            jax.ShapeDtypeStruct((rows // 128, 128), F32),
        ),
        cost_estimate=pl.CostEstimate(
            flops=8 * rows * rows, bytes_accessed=2 * rows * rows, transcendentals=0),
        compiler_params=roomy(8),
        name="place",
    )(
        me,
        map_lanes,
        cond_index.reshape(-1, 128),
        val_index.reshape(-1, 128),
        cond_energy.reshape(-1, 128),
        val_energy.reshape(-1, 128),
    )

    if per_peer % 128 != 0:
        arrived = jnp.sum(arrived.reshape(n // 2, 2, m, half, 2 * per_peer).astype(F32), axis=2).astype(BF16)
        arrived = arrived.transpose(1, 2, 0, 3).reshape(2, half, rows)
    parts, layers = (n, m) if per_peer % 128 == 0 else (2, 1)
    response = pl.pallas_call(
        lambda *refs: final_kernel(parts, layers, *refs),
        in_specs=[WHOLE] * 4,
        out_specs=WHOLE,
        compiler_params=roomy(8),
        out_shape=jax.ShapeDtypeStruct((vecs, rows), BF16),
        scratch_shapes=[pltpu.VMEM((vecs, rows), BF16)],
        cost_estimate=pl.CostEstimate(
            flops=2 * rows * rows * vecs, bytes_accessed=2 * rows * rows, transcendentals=0),
        name="final",
    )(arrived, place, gap, trial_rows.T)
    return (response.T, tiles)


def solution(mesh):
    in_specs = (
        P("pairs", "rep"),
        P("pairs", "rep"),
        P("rep"),
        P("pairs", "rep"),
        P("pairs", "rep"),
        P(),
        P("pairs"),
        P("pairs"),
        P(),
        P(),
    )
    out_specs = (P("pairs", "rep"), P("rep", "pairs", None))

    return jax.shard_map(per_device, mesh=mesh, in_specs=in_specs, out_specs=out_specs, check_vma=False)
```

```python
import jax
import jax.numpy as jnp
from jax import lax
from jax.experimental import pallas as pl
from jax.experimental.pallas import tpu as pltpu
from jax.sharding import PartitionSpec as P

F32 = jnp.float32
BF16 = jnp.bfloat16
SCALAR = pl.BlockSpec(memory_space=pltpu.SMEM)
WHOLE = pl.BlockSpec(memory_space=pltpu.VMEM)


def roomy(mib):
    return pltpu.CompilerParams(vmem_limit_bytes=mib << 20)


def exchange(x, mask):
    size = lax.axis_size("pairs")
    return lax.ppermute(x, "pairs", [(i, i ^ mask) for i in range(size)])


def in_order(odd, own, partner):
    return jnp.where(odd, jnp.stack([partner, own]), jnp.stack([own, partner]))


def lane_cumsum(x):
    width = x.shape[1]
    lane = lax.broadcasted_iota(jnp.int32, x.shape, 1)
    step = 1
    while step < width:
        x = x + jnp.where(lane >= step, pltpu.roll(x, step, 1), 0)
        step *= 2
    return x


def lookup(table_ref, index):
    value = jnp.zeros(index.shape, F32)
    for part in range(table_ref.shape[0]):
        row = jnp.broadcast_to(table_ref[part : part + 1, :], index.shape)
        near = jnp.clip(index - 128 * part, 0, 127)
        found = jnp.take_along_axis(row, near, axis=1)
        value = jnp.where(index // 128 == part, found, value)
    return value


def load_kernel(n, me_ref, map_hbm, val_hbm, screen_hbm, scaled_ref, order_ref, screen_ref, map_ref, val_ref, sems):
    rows = val_ref.shape[0]
    per_peer = rows // n
    lanes = rows // 128
    parts = 4
    tall = rows // parts
    first = pl.multiple_of((me_ref[0] // 2) * (2 * lanes), lanes)
    head = [
        pltpu.make_async_copy(screen_hbm, screen_ref, sems.at[0]),
        pltpu.make_async_copy(map_hbm.at[pl.ds(first, 2 * lanes), :], map_ref, sems.at[1]),
    ]
    body = [
        pltpu.make_async_copy(
            val_hbm.at[pl.ds(k * tall, tall), :], val_ref.at[pl.ds(k * tall, tall), :], sems.at[2 + k])
        for k in range(parts)
    ]
    for copy in head + body:
        copy.start()
    for copy in head:
        copy.wait()
    block = lax.broadcasted_iota(jnp.int32, (n, rows), 0)
    for flip in range(2):
        at = pl.multiple_of(((me_ref[0] & 1) ^ flip) * lanes, lanes)
        own = map_ref[pl.ds(at, lanes), :]
        own = jnp.concatenate([own[c : c + 1, :] for c in range(lanes)], axis=1)
        own = jnp.broadcast_to(own, (n, rows))
        goes = (own >= block * rows) & (own < (block + 1) * rows)
        rank = lane_cumsum(goes.astype(jnp.int32)) - 1
        order_ref[flip : flip + 1, :] = jnp.sum(
            jnp.where(goes, rank + block * per_peer, 0), axis=0, keepdims=True)
    for k, copy in enumerate(body):
        copy.wait()
        part = slice(k * tall, (k + 1) * tall)
        scaled_ref[part, :] = (val_ref[part, :].astype(F32) * screen_ref[...]).astype(BF16)


def fetch_kernel(trial_hbm, cond_hbm, trial_ref, cond_ref, sems):
    copies = [
        pltpu.make_async_copy(trial_hbm, trial_ref, sems.at[0]),
        pltpu.make_async_copy(cond_hbm, cond_ref, sems.at[1]),
    ]
    for copy in copies:
        copy.start()
    for copy in copies:
        copy.wait()


def send_order(order, scaled, sent_ref):
    rows = sent_ref.shape[0]
    chunk = 128
    for c in range(rows // chunk):
        ids = lax.broadcasted_iota(jnp.int32, (chunk, rows), 0) + c * chunk
        pick = jnp.where(ids == order, 1.0, 0.0).astype(BF16)
        sent_ref[c * chunk : (c + 1) * chunk, :] = jnp.dot(
            pick, scaled, preferred_element_type=F32
        ).astype(BF16)


def sent_kernel(order_ref, scaled_ref, sent_ref):
    send_order(order_ref[0:1, :], scaled_ref[...], sent_ref)


def other_kernel(order_ref, screen_ref, val_ref, sent_ref):
    scaled = (val_ref[...].astype(F32) * screen_ref[...]).astype(BF16)
    send_order(order_ref[1:2, :], scaled, sent_ref)


def place_kernel(n, rows, me_ref, map_ref, ci_ref, vi_ref, ce_ref, ve_ref, slot_ref, gap_ref):
    per_peer = rows // n
    lanes = rows // 128
    gap_ref[...] = lookup(ce_ref, ci_ref[...]) - lookup(ve_ref, vi_ref[...])
    grid = jnp.concatenate([map_ref[pl.ds(c, n, stride=lanes), :] for c in range(lanes)], axis=1)
    slots = grid - me_ref[0] * rows
    lands = (slots >= 0) & (slots < rows)
    arrival = jnp.where(lands, lane_cumsum(lands.astype(jnp.int32)) - 1, -1)
    slots = slots.astype(F32)
    ids = lax.broadcasted_iota(jnp.int32, (per_peer, rows), 0)
    for q in range(n):
        hit = ids == arrival[q : q + 1, :]
        slot = jnp.sum(jnp.where(hit, slots[q : q + 1, :], 0.0), axis=1, keepdims=True)
        slot_ref[q * per_peer : (q + 1) * per_peer, :] = jnp.broadcast_to(slot, (per_peer, 128))


def tile_kernel(me_ref, val_ref, screen_ref, mine_ref, theirs_ref, out_ref):
    scaled = (val_ref[...].astype(F32) * screen_ref[...]).astype(BF16)
    chips, cols, _ = mine_ref.shape
    me = me_ref[0]
    for k in range(chips):
        for flip, cond_ref in enumerate((mine_ref, theirs_ref)):
            tile = lax.dot_general(
                scaled, cond_ref[k], (((1,), (1,)), ((), ())), preferred_element_type=F32
            )
            start = pl.multiple_of((me ^ (2 * k + flip)) * cols, 128)
            out_ref[0, :, pl.ds(start, cols)] = tile.astype(BF16)


def mixed_kernel(m, me_ref, vec_ref, cond_ref, keep_ref, give_ref):
    chips, vecs, cols = vec_ref.shape
    depth = cond_ref.shape[-1]
    odd = (me_ref[0] & 1) == 1
    vec = jnp.concatenate([vec_ref[k] for k in range(chips)], axis=1)
    total = jnp.dot(vec, cond_ref[...].reshape(chips * cols, depth), preferred_element_type=F32)
    half = vecs // (2 * m)
    for k in range(m):
        low = total[2 * k * half : (2 * k + 1) * half]
        high = total[(2 * k + 1) * half : (2 * k + 2) * half]
        keep_ref[k * half : (k + 1) * half, :] = jnp.where(odd, high, low)
        give_ref[k * half : (k + 1) * half, :] = jnp.where(odd, low, high).astype(BF16)


def apply_kernel(m, n, me_ref, keep_ref, take_ref, own_ref, other_ref, out_ref):
    half, width = out_ref.shape[1:]
    per_peer = width // 2
    odd = (me_ref[0] & 1) == 1
    mixed = (keep_ref[...] + take_ref[...].astype(F32)).astype(BF16)
    rows_last = (((1,), (1,)), ((), ()))
    own, other = (
        lax.dot_general(mixed, ref[...], rows_last, preferred_element_type=F32).astype(BF16)
        for ref in (own_ref, other_ref)
    )
    first, second = jnp.where(odd, other, own), jnp.where(odd, own, other)
    for d in range(n):
        at = slice(d * per_peer, (d + 1) * per_peer)
        for k in range(m):
            out_ref[d * m + k, :, :per_peer] = first[k * half : (k + 1) * half, at]
            out_ref[d * m + k, :, per_peer:] = second[k * half : (k + 1) * half, at]


def final_kernel(n, m, arrived_ref, slot_ref, gap_ref, trial_ref, out_ref, row_ref):
    width = out_ref.shape[1]
    half, pair = arrived_ref.shape[1:]
    for q in range(n):
        total = arrived_ref[q * m].astype(F32)
        for k in range(1, m):
            total = total + arrived_ref[q * m + k].astype(F32)
        at = (q & 1) * half
        row_ref[at : at + half, (q // 2) * pair : (q // 2 + 1) * pair] = total.astype(BF16)
    slot = slot_ref[...]
    lane = lax.broadcasted_iota(jnp.int32, slot.shape, 1).astype(F32)
    for c in range(0, width // 128, 2):
        lands = jnp.concatenate(
            [jnp.where(slot == lane + 128.0 * (c + k), 1.0, 0.0).astype(BF16) for k in range(2)], axis=1)
        moved = jnp.dot(row_ref[...], lands, preferred_element_type=F32)
        for k in range(2):
            part = slice((c + k) * 128, (c + k + 1) * 128)
            gap = gap_ref[c + k : c + k + 1, :]
            out_ref[:, part] = (
                gap * trial_ref[:, part].astype(F32) + moved[:, k * 128 : (k + 1) * 128]
            ).astype(BF16)


def per_device(
    mat_val,
    mat_cond,
    screening,
    trial_cols,
    trial_rows,
    row_map,
    val_index,
    cond_index,
    val_energy,
    cond_energy,
):
    n = lax.axis_size("pairs")
    m = lax.axis_size("rep")
    rows, depth = mat_val.shape
    cols = mat_cond.shape[0]
    vecs = trial_cols.shape[1]
    half = vecs // 2
    per_peer = rows // n
    own = lax.axis_index("pairs").astype(jnp.int32)
    layer = lax.axis_index("rep").astype(jnp.int32)
    odd = (own & 1) == 1
    me = own.reshape(1)
    screen = screening.reshape(1, depth)
    map_lanes = row_map.reshape(-1, 128)

    far_away = pl.BlockSpec(memory_space=pltpu.HBM)

    def in_hbm(x):
        return pltpu.with_memory_space_constraint(x, pltpu.HBM)

    val_other = exchange(mat_val, 1)
    trial, cond_own = pl.pallas_call(
        fetch_kernel,
        in_specs=[far_away, far_away],
        out_specs=(WHOLE, WHOLE),
        out_shape=(
            jax.ShapeDtypeStruct((vecs, cols), BF16),
            jax.ShapeDtypeStruct((cols, depth), BF16),
        ),
        scratch_shapes=[pltpu.SemaphoreType.DMA((2,))],
        cost_estimate=pl.CostEstimate(flops=0, bytes_accessed=4 * cols * depth, transcendentals=0),
        compiler_params=roomy(4),
        name="fetch",
    )(in_hbm(trial_cols.T), in_hbm(mat_cond))
    turns = [trial]
    for k in range(1, m):
        turns.append(lax.ppermute(trial_cols.T, "rep", [(i, (i + k) % m) for i in range(m)]))
    wide = []
    for k in range(m):
        block = turns[0]
        for t in range(1, m):
            block = jnp.where(lax.rem(layer - t + m, m) == k, turns[t], block)
        wide.append(block)
    wide = jnp.concatenate(wide)
    vec_all = jnp.stack([wide] + [exchange(wide, k) for k in range(2, n, 2)])
    mine = jnp.stack([cond_own] + [exchange(mat_cond, k) for k in range(2, n, 2)])
    theirs = exchange(mine, 1)
    scaled, order, screen_near = pl.pallas_call(
        lambda *refs: load_kernel(n, *refs),
        in_specs=[SCALAR] + [far_away] * 3,
        out_specs=(WHOLE, WHOLE, WHOLE),
        out_shape=(
            jax.ShapeDtypeStruct((rows, depth), BF16),
            jax.ShapeDtypeStruct((2, rows), jnp.int32),
            jax.ShapeDtypeStruct((1, depth), F32),
        ),
        scratch_shapes=[
            pltpu.VMEM((2 * rows // 128, 128), jnp.int32),
            pltpu.VMEM((rows, depth), BF16),
            pltpu.SemaphoreType.DMA((6,)),
        ],
        cost_estimate=pl.CostEstimate(flops=rows * depth, bytes_accessed=4 * rows * depth, transcendentals=0),
        compiler_params=roomy(8),
        name="load",
    )(me, in_hbm(map_lanes), in_hbm(mat_val), in_hbm(screen))
    sent_cost = pl.CostEstimate(
        flops=2 * rows * rows * depth, bytes_accessed=4 * rows * depth, transcendentals=0)
    sent = [
        pl.pallas_call(
            body,
            in_specs=[WHOLE] * len(given),
            out_specs=WHOLE,
            out_shape=jax.ShapeDtypeStruct((rows, depth), BF16),
            cost_estimate=sent_cost,
            compiler_params=roomy(6),
        )(*given)
        for body, given in ((sent_kernel, (order, scaled)), (other_kernel, (order, screen_near, val_other)))
    ]
    keep, give = pl.pallas_call(
        lambda *refs: mixed_kernel(m, *refs),
        in_specs=[SCALAR, WHOLE, WHOLE],
        out_specs=(WHOLE, WHOLE),
        out_shape=(
            jax.ShapeDtypeStruct((m * half, depth), F32),
            jax.ShapeDtypeStruct((m * half, depth), BF16),
        ),
        cost_estimate=pl.CostEstimate(
            flops=2 * m * vecs * n * cols * depth // 2, bytes_accessed=n * cols * depth, transcendentals=0),
        compiler_params=roomy(8),
        name="mixed",
    )(me, vec_all, mine)
    take = exchange(give, 1)

    if per_peer % 128 == 0:
        outgoing = pl.pallas_call(
            lambda *refs: apply_kernel(m, n, *refs),
            in_specs=[SCALAR] + [WHOLE] * 4,
            out_specs=WHOLE,
            compiler_params=roomy(8),
            out_shape=jax.ShapeDtypeStruct((n * m, half, 2 * per_peer), BF16),
            cost_estimate=pl.CostEstimate(
                flops=4 * rows * depth * m * half, bytes_accessed=4 * rows * depth, transcendentals=0),
            name="apply",
        )(me, keep, take, *sent)
    else:
        mixed = (keep + take.astype(F32)).astype(BF16)
        partial = jnp.einsum("vg,srg->svr", mixed, jnp.stack(sent), preferred_element_type=F32).astype(BF16)
        partial = in_order(odd, partial[0], partial[1]).reshape(2, m, half, n, per_peer)
        outgoing = partial.transpose(3, 1, 2, 0, 4).reshape(n * m, half, 2 * per_peer)
    arrived = lax.all_to_all(outgoing, ("pairs", "rep"), split_axis=0, concat_axis=0, tiled=True)

    tall = min(rows, 256)
    tiles = pl.pallas_call(
        tile_kernel,
        grid_spec=pltpu.PrefetchScalarGridSpec(
            num_scalar_prefetch=1,
            grid=(rows // tall,),
            in_specs=[
                pl.BlockSpec((tall, depth), lambda d, me: (d, 0)),
                pl.BlockSpec((1, depth), lambda d, me: (0, 0)),
                pl.BlockSpec((n // 2, cols, depth), lambda d, me: (0, 0, 0)),
                pl.BlockSpec((n // 2, cols, depth), lambda d, me: (0, 0, 0)),
            ],
            out_specs=pl.BlockSpec((1, tall, n * cols), lambda d, me: (0, d, 0)),
        ),
        out_shape=jax.ShapeDtypeStruct((1, rows, n * cols), BF16),
        cost_estimate=pl.CostEstimate(
            flops=2 * rows * depth * n * cols, bytes_accessed=2 * rows * (depth + n * cols), transcendentals=0),
        compiler_params=roomy(8),
        name="tiles",
    )(me, mat_val, screen, mine, theirs)

    slot, gap = pl.pallas_call(
        lambda *refs: place_kernel(n, rows, *refs),
        in_specs=[SCALAR] + [WHOLE] * 5,
        out_specs=(WHOLE, WHOLE),
        out_shape=(
            jax.ShapeDtypeStruct((rows, 128), F32),
            jax.ShapeDtypeStruct((rows // 128, 128), F32),
        ),
        cost_estimate=pl.CostEstimate(
            flops=8 * rows * rows, bytes_accessed=2 * rows * rows, transcendentals=0),
        compiler_params=roomy(8),
        name="place",
    )(
        me,
        map_lanes,
        cond_index.reshape(-1, 128),
        val_index.reshape(-1, 128),
        cond_energy.reshape(-1, 128),
        val_energy.reshape(-1, 128),
    )

    if per_peer % 128 != 0:
        arrived = jnp.sum(arrived.reshape(n // 2, 2, m, half, 2 * per_peer).astype(F32), axis=2).astype(BF16)
        arrived = arrived.transpose(1, 2, 0, 3).reshape(2, half, rows)
    parts, layers = (n, m) if per_peer % 128 == 0 else (2, 1)
    response = pl.pallas_call(
        lambda *refs: final_kernel(parts, layers, *refs),
        in_specs=[WHOLE] * 4,
        out_specs=WHOLE,
        compiler_params=roomy(8),
        out_shape=jax.ShapeDtypeStruct((vecs, rows), BF16),
        scratch_shapes=[pltpu.VMEM((vecs, rows), BF16)],
        cost_estimate=pl.CostEstimate(
            flops=2 * rows * rows * vecs, bytes_accessed=2 * rows * rows, transcendentals=0),
        name="final",
    )(arrived, slot, gap, trial_rows.T)
    return (response.T, tiles)


def solution(mesh):
    in_specs = (
        P("pairs", "rep"),
        P("pairs", "rep"),
        P("rep"),
        P("pairs", "rep"),
        P("pairs", "rep"),
        P(),
        P("pairs"),
        P("pairs"),
        P(),
        P(),
    )
    out_specs = (P("pairs", "rep"), P("rep", "pairs", None))

    return jax.shard_map(per_device, mesh=mesh, in_specs=in_specs, out_specs=out_specs, check_vma=False)
```

```python
import jax
import jax.numpy as jnp
from jax import lax
from jax.experimental import pallas as pl
from jax.experimental.pallas import tpu as pltpu
from jax.sharding import PartitionSpec as P

F32 = jnp.float32
BF16 = jnp.bfloat16
SCALAR = pl.BlockSpec(memory_space=pltpu.SMEM)
WHOLE = pl.BlockSpec(memory_space=pltpu.VMEM)


def roomy(mib):
    return pltpu.CompilerParams(vmem_limit_bytes=mib << 20)


def exchange(x, mask):
    size = lax.axis_size("pairs")
    return lax.ppermute(x, "pairs", [(i, i ^ mask) for i in range(size)])


def in_order(odd, own, partner):
    return jnp.where(odd, jnp.stack([partner, own]), jnp.stack([own, partner]))


def lane_cumsum(x):
    width = x.shape[1]
    lane = lax.broadcasted_iota(jnp.int32, x.shape, 1)
    step = 1
    while step < width:
        x = x + jnp.where(lane >= step, pltpu.roll(x, step, 1), 0)
        step *= 2
    return x


def lookup(table_ref, index):
    value = jnp.zeros(index.shape, F32)
    for part in range(table_ref.shape[0]):
        row = jnp.broadcast_to(table_ref[part : part + 1, :], index.shape)
        near = jnp.clip(index - 128 * part, 0, 127)
        found = jnp.take_along_axis(row, near, axis=1)
        value = jnp.where(index // 128 == part, found, value)
    return value


def load_kernel(n, me_ref, map_hbm, val_hbm, screen_hbm, scaled_ref, order_ref, screen_ref, map_ref, val_ref, sems):
    rows = val_ref.shape[0]
    per_peer = rows // n
    lanes = rows // 128
    parts = 4
    tall = rows // parts
    first = pl.multiple_of((me_ref[0] // 2) * (2 * lanes), lanes)
    head = [
        pltpu.make_async_copy(screen_hbm, screen_ref, sems.at[0]),
        pltpu.make_async_copy(map_hbm.at[pl.ds(first, 2 * lanes), :], map_ref, sems.at[1]),
    ]
    body = [
        pltpu.make_async_copy(
            val_hbm.at[pl.ds(k * tall, tall), :], val_ref.at[pl.ds(k * tall, tall), :], sems.at[2 + k])
        for k in range(parts)
    ]
    for copy in head + body:
        copy.start()
    for copy in head:
        copy.wait()
    block = lax.broadcasted_iota(jnp.int32, (n, rows), 0)
    for flip in range(2):
        at = pl.multiple_of(((me_ref[0] & 1) ^ flip) * lanes, lanes)
        own = map_ref[pl.ds(at, lanes), :]
        own = jnp.concatenate([own[c : c + 1, :] for c in range(lanes)], axis=1)
        own = jnp.broadcast_to(own, (n, rows))
        goes = (own >= block * rows) & (own < (block + 1) * rows)
        rank = lane_cumsum(goes.astype(jnp.int32)) - 1
        order_ref[flip : flip + 1, :] = jnp.sum(
            jnp.where(goes, rank + block * per_peer, 0), axis=0, keepdims=True)
    for k, copy in enumerate(body):
        copy.wait()
        part = slice(k * tall, (k + 1) * tall)
        scaled_ref[part, :] = (val_ref[part, :].astype(F32) * screen_ref[...]).astype(BF16)


def fetch_kernel(trial_hbm, cond_hbm, trial_ref, cond_ref, sems):
    copies = [
        pltpu.make_async_copy(trial_hbm, trial_ref, sems.at[0]),
        pltpu.make_async_copy(cond_hbm, cond_ref, sems.at[1]),
    ]
    for copy in copies:
        copy.start()
    for copy in copies:
        copy.wait()


def send_order(order, scaled, sent_ref):
    rows = sent_ref.shape[0]
    chunk = 128
    for c in range(rows // chunk):
        ids = lax.broadcasted_iota(jnp.int32, (chunk, rows), 0) + c * chunk
        pick = jnp.where(ids == order, 1.0, 0.0).astype(BF16)
        sent_ref[c * chunk : (c + 1) * chunk, :] = jnp.dot(
            pick, scaled, preferred_element_type=F32
        ).astype(BF16)


def sent_kernel(order_ref, scaled_ref, sent_ref):
    send_order(order_ref[0:1, :], scaled_ref[...], sent_ref)


def other_kernel(parity, me_ref, order_ref, screen_ref, val_ref, *refs):
    @pl.when((me_ref[0] & 1) == parity)
    def _():
        scaled = (val_ref[...].astype(F32) * screen_ref[...]).astype(BF16)
        send_order(order_ref[1:2, :], scaled, refs[-1])


def place_kernel(n, rows, me_ref, map_ref, ci_ref, vi_ref, ce_ref, ve_ref, slot_ref, gap_ref):
    per_peer = rows // n
    lanes = rows // 128
    gap_ref[...] = lookup(ce_ref, ci_ref[...]) - lookup(ve_ref, vi_ref[...])
    grid = jnp.concatenate([map_ref[pl.ds(c, n, stride=lanes), :] for c in range(lanes)], axis=1)
    slots = grid - me_ref[0] * rows
    lands = (slots >= 0) & (slots < rows)
    arrival = jnp.where(lands, lane_cumsum(lands.astype(jnp.int32)) - 1, -1)
    slots = slots.astype(F32)
    ids = lax.broadcasted_iota(jnp.int32, (per_peer, rows), 0)
    for q in range(n):
        hit = ids == arrival[q : q + 1, :]
        slot = jnp.sum(jnp.where(hit, slots[q : q + 1, :], 0.0), axis=1, keepdims=True)
        slot_ref[q * per_peer : (q + 1) * per_peer, :] = jnp.broadcast_to(slot, (per_peer, 128))


def tile_kernel(me_ref, val_ref, screen_ref, mine_ref, theirs_ref, out_ref):
    scaled = (val_ref[...].astype(F32) * screen_ref[...]).astype(BF16)
    chips, cols, _ = mine_ref.shape
    me = me_ref[0]
    for k in range(chips):
        for flip, cond_ref in enumerate((mine_ref, theirs_ref)):
            tile = lax.dot_general(
                scaled, cond_ref[k], (((1,), (1,)), ((), ())), preferred_element_type=F32
            )
            start = pl.multiple_of((me ^ (2 * k + flip)) * cols, 128)
            out_ref[0, :, pl.ds(start, cols)] = tile.astype(BF16)


def mixed_kernel(m, me_ref, vec_ref, cond_ref, keep_ref, give_ref):
    chips, vecs, cols = vec_ref.shape
    depth = cond_ref.shape[-1]
    odd = (me_ref[0] & 1) == 1
    vec = jnp.concatenate([vec_ref[k] for k in range(chips)], axis=1)
    total = jnp.dot(vec, cond_ref[...].reshape(chips * cols, depth), preferred_element_type=F32)
    half = vecs // (2 * m)
    for k in range(m):
        low = total[2 * k * half : (2 * k + 1) * half]
        high = total[(2 * k + 1) * half : (2 * k + 2) * half]
        keep_ref[k * half : (k + 1) * half, :] = jnp.where(odd, high, low)
        give_ref[k * half : (k + 1) * half, :] = jnp.where(odd, low, high).astype(BF16)


def apply_kernel(m, n, me_ref, keep_ref, take_ref, own_ref, other_ref, out_hbm, out_ref, sems):
    half, width = out_ref.shape[1:]
    per_peer = width // 2
    odd = (me_ref[0] & 1) == 1
    mixed = (keep_ref[...] + take_ref[...].astype(F32)).astype(BF16)
    shares = sems.shape[0]
    tall = own_ref.shape[0] // shares
    blocks = (n // shares) * m
    copies = []
    for share in range(shares):
        part = slice(share * tall, (share + 1) * tall)
        own, other = (
            lax.dot_general(
                mixed, ref[part, :], (((1,), (1,)), ((), ())), preferred_element_type=F32
            ).astype(BF16)
            for ref in (own_ref, other_ref)
        )
        first, second = jnp.where(odd, other, own), jnp.where(odd, own, other)
        for d in range(n // shares):
            at = slice(d * per_peer, (d + 1) * per_peer)
            for k in range(m):
                to = share * blocks + d * m + k
                out_ref[to, :, :per_peer] = first[k * half : (k + 1) * half, at]
                out_ref[to, :, per_peer:] = second[k * half : (k + 1) * half, at]
        some = pl.ds(share * blocks, blocks)
        copies.append(pltpu.make_async_copy(out_ref.at[some], out_hbm.at[some], sems.at[share]))
        copies[-1].start()
    for copy in copies:
        copy.wait()


def final_kernel(n, m, arrived_ref, slot_ref, gap_ref, trial_ref, out_ref, row_ref):
    width = out_ref.shape[1]
    half, pair = arrived_ref.shape[1:]
    for q in range(n):
        total = arrived_ref[q * m].astype(F32)
        for k in range(1, m):
            total = total + arrived_ref[q * m + k].astype(F32)
        at = (q & 1) * half
        row_ref[at : at + half, (q // 2) * pair : (q // 2 + 1) * pair] = total.astype(BF16)
    slot = slot_ref[...]
    lane = lax.broadcasted_iota(jnp.int32, slot.shape, 1).astype(F32)
    for c in range(0, width // 128, 2):
        lands = jnp.concatenate(
            [jnp.where(slot == lane + 128.0 * (c + k), 1.0, 0.0).astype(BF16) for k in range(2)], axis=1)
        moved = jnp.dot(row_ref[...], lands, preferred_element_type=F32)
        for k in range(2):
            part = slice((c + k) * 128, (c + k + 1) * 128)
            gap = gap_ref[c + k : c + k + 1, :]
            out_ref[:, part] = (
                gap * trial_ref[:, part].astype(F32) + moved[:, k * 128 : (k + 1) * 128]
            ).astype(BF16)


def per_device(
    mat_val,
    mat_cond,
    screening,
    trial_cols,
    trial_rows,
    row_map,
    val_index,
    cond_index,
    val_energy,
    cond_energy,
):
    n = lax.axis_size("pairs")
    m = lax.axis_size("rep")
    rows, depth = mat_val.shape
    cols = mat_cond.shape[0]
    vecs = trial_cols.shape[1]
    half = vecs // 2
    per_peer = rows // n
    own = lax.axis_index("pairs").astype(jnp.int32)
    layer = lax.axis_index("rep").astype(jnp.int32)
    odd = (own & 1) == 1
    me = own.reshape(1)
    screen = screening.reshape(1, depth)
    map_lanes = row_map.reshape(-1, 128)

    far_away = pl.BlockSpec(memory_space=pltpu.HBM)

    def in_hbm(x):
        return pltpu.with_memory_space_constraint(x, pltpu.HBM)

    val_other = exchange(mat_val, 1)
    trial, cond_own = pl.pallas_call(
        fetch_kernel,
        in_specs=[far_away, far_away],
        out_specs=(WHOLE, WHOLE),
        out_shape=(
            jax.ShapeDtypeStruct((vecs, cols), BF16),
            jax.ShapeDtypeStruct((cols, depth), BF16),
        ),
        scratch_shapes=[pltpu.SemaphoreType.DMA((2,))],
        cost_estimate=pl.CostEstimate(flops=0, bytes_accessed=4 * cols * depth, transcendentals=0),
        compiler_params=roomy(4),
        name="fetch",
    )(in_hbm(trial_cols.T), in_hbm(mat_cond))
    turns = [trial]
    for k in range(1, m):
        turns.append(lax.ppermute(trial_cols.T, "rep", [(i, (i + k) % m) for i in range(m)]))
    wide = []
    for k in range(m):
        block = turns[0]
        for t in range(1, m):
            block = jnp.where(lax.rem(layer - t + m, m) == k, turns[t], block)
        wide.append(block)
    wide = jnp.concatenate(wide)
    vec_all = jnp.stack([wide] + [exchange(wide, k) for k in range(2, n, 2)])
    mine = jnp.stack([cond_own] + [exchange(mat_cond, k) for k in range(2, n, 2)])
    theirs = exchange(mine, 1)
    scaled, order, screen_near = pl.pallas_call(
        lambda *refs: load_kernel(n, *refs),
        in_specs=[SCALAR] + [far_away] * 3,
        out_specs=(WHOLE, WHOLE, WHOLE),
        out_shape=(
            jax.ShapeDtypeStruct((rows, depth), BF16),
            jax.ShapeDtypeStruct((2, rows), jnp.int32),
            jax.ShapeDtypeStruct((1, depth), F32),
        ),
        scratch_shapes=[
            pltpu.VMEM((2 * rows // 128, 128), jnp.int32),
            pltpu.VMEM((rows, depth), BF16),
            pltpu.SemaphoreType.DMA((6,)),
        ],
        cost_estimate=pl.CostEstimate(flops=rows * depth, bytes_accessed=4 * rows * depth, transcendentals=0),
        compiler_params=roomy(8),
        name="load",
    )(me, in_hbm(map_lanes), in_hbm(mat_val), in_hbm(screen))
    sent_cost = pl.CostEstimate(
        flops=2 * rows * rows * depth, bytes_accessed=4 * rows * depth, transcendentals=0)
    sent_shape = jax.ShapeDtypeStruct((rows, depth), BF16)
    sent = pl.pallas_call(
        sent_kernel,
        in_specs=[WHOLE] * 2,
        out_specs=WHOLE,
        out_shape=sent_shape,
        cost_estimate=sent_cost,
        compiler_params=roomy(6),
        name="sent0",
    )(order, scaled)
    sent_other = ()
    for parity in (1, 0):
        sent_other = (pl.pallas_call(
            lambda *refs, parity=parity: other_kernel(parity, *refs),
            in_specs=[SCALAR] + [WHOLE] * (3 + len(sent_other)),
            out_specs=WHOLE,
            out_shape=sent_shape,
            input_output_aliases={4: 0} if sent_other else {},
            cost_estimate=sent_cost,
            compiler_params=roomy(6),
        )(me, order, screen_near, val_other, *sent_other),)
    sent = (sent, *sent_other)
    keep, give = pl.pallas_call(
        lambda *refs: mixed_kernel(m, *refs),
        in_specs=[SCALAR, WHOLE, WHOLE],
        out_specs=(WHOLE, WHOLE),
        out_shape=(
            jax.ShapeDtypeStruct((m * half, depth), F32),
            jax.ShapeDtypeStruct((m * half, depth), BF16),
        ),
        cost_estimate=pl.CostEstimate(
            flops=2 * m * vecs * n * cols * depth // 2, bytes_accessed=n * cols * depth, transcendentals=0),
        compiler_params=roomy(8),
        name="mixed",
    )(me, vec_all, mine)
    take = exchange(give, 1)

    if per_peer % 128 == 0:
        outgoing = pl.pallas_call(
            lambda *refs: apply_kernel(m, n, *refs),
            in_specs=[SCALAR] + [WHOLE] * 4,
            out_specs=pl.BlockSpec(memory_space=pltpu.HBM),
            scratch_shapes=[
                pltpu.VMEM((n * m, half, 2 * per_peer), BF16),
                pltpu.SemaphoreType.DMA((2,)),
            ],
            compiler_params=roomy(8),
            out_shape=jax.ShapeDtypeStruct((n * m, half, 2 * per_peer), BF16),
            cost_estimate=pl.CostEstimate(
                flops=4 * rows * depth * m * half, bytes_accessed=4 * rows * depth, transcendentals=0),
            name="apply",
        )(me, keep, take, *sent)
    else:
        mixed = (keep + take.astype(F32)).astype(BF16)
        partial = jnp.einsum("vg,srg->svr", mixed, jnp.stack(sent), preferred_element_type=F32).astype(BF16)
        partial = in_order(odd, partial[0], partial[1]).reshape(2, m, half, n, per_peer)
        outgoing = partial.transpose(3, 1, 2, 0, 4).reshape(n * m, half, 2 * per_peer)
    arrived = lax.all_to_all(outgoing, ("pairs", "rep"), split_axis=0, concat_axis=0, tiled=True)

    tall = min(rows, 256)
    tiles = pl.pallas_call(
        tile_kernel,
        grid_spec=pltpu.PrefetchScalarGridSpec(
            num_scalar_prefetch=1,
            grid=(rows // tall,),
            in_specs=[
                pl.BlockSpec((tall, depth), lambda d, me: (d, 0)),
                pl.BlockSpec((1, depth), lambda d, me: (0, 0)),
                pl.BlockSpec((n // 2, cols, depth), lambda d, me: (0, 0, 0)),
                pl.BlockSpec((n // 2, cols, depth), lambda d, me: (0, 0, 0)),
            ],
            out_specs=pl.BlockSpec((1, tall, n * cols), lambda d, me: (0, d, 0)),
        ),
        out_shape=jax.ShapeDtypeStruct((1, rows, n * cols), BF16),
        cost_estimate=pl.CostEstimate(
            flops=2 * rows * depth * n * cols, bytes_accessed=2 * rows * (depth + n * cols), transcendentals=0),
        compiler_params=roomy(8),
        name="tiles",
    )(me, mat_val, screen, mine, theirs)

    slot, gap = pl.pallas_call(
        lambda *refs: place_kernel(n, rows, *refs),
        in_specs=[SCALAR] + [WHOLE] * 5,
        out_specs=(WHOLE, WHOLE),
        out_shape=(
            jax.ShapeDtypeStruct((rows, 128), F32),
            jax.ShapeDtypeStruct((rows // 128, 128), F32),
        ),
        cost_estimate=pl.CostEstimate(
            flops=8 * rows * rows, bytes_accessed=2 * rows * rows, transcendentals=0),
        compiler_params=roomy(8),
        name="place",
    )(
        me,
        map_lanes,
        cond_index.reshape(-1, 128),
        val_index.reshape(-1, 128),
        cond_energy.reshape(-1, 128),
        val_energy.reshape(-1, 128),
    )

    if per_peer % 128 != 0:
        arrived = jnp.sum(arrived.reshape(n // 2, 2, m, half, 2 * per_peer).astype(F32), axis=2).astype(BF16)
        arrived = arrived.transpose(1, 2, 0, 3).reshape(2, half, rows)
    parts, layers = (n, m) if per_peer % 128 == 0 else (2, 1)
    response = pl.pallas_call(
        lambda *refs: final_kernel(parts, layers, *refs),
        in_specs=[WHOLE] * 4,
        out_specs=WHOLE,
        compiler_params=roomy(8),
        out_shape=jax.ShapeDtypeStruct((vecs, rows), BF16),
        scratch_shapes=[pltpu.VMEM((vecs, rows), BF16)],
        cost_estimate=pl.CostEstimate(
            flops=2 * rows * rows * vecs, bytes_accessed=2 * rows * rows, transcendentals=0),
        name="final",
    )(arrived, slot, gap, trial_rows.T)
    return (response.T, tiles)


def solution(mesh):
    in_specs = (
        P("pairs", "rep"),
        P("pairs", "rep"),
        P("rep"),
        P("pairs", "rep"),
        P("pairs", "rep"),
        P(),
        P("pairs"),
        P("pairs"),
        P(),
        P(),
    )
    out_specs = (P("pairs", "rep"), P("rep", "pairs", None))

    return jax.shard_map(per_device, mesh=mesh, in_specs=in_specs, out_specs=out_specs, check_vma=False)
```

```python
import jax
import jax.numpy as jnp
from jax import lax
from jax.experimental import pallas as pl
from jax.experimental.pallas import tpu as pltpu
from jax.sharding import PartitionSpec as P

F32 = jnp.float32
BF16 = jnp.bfloat16
SCALAR = pl.BlockSpec(memory_space=pltpu.SMEM)
WHOLE = pl.BlockSpec(memory_space=pltpu.VMEM)


def roomy(mib):
    return pltpu.CompilerParams(vmem_limit_bytes=mib << 20)


def exchange(x, mask):
    size = lax.axis_size("pairs")
    return lax.ppermute(x, "pairs", [(i, i ^ mask) for i in range(size)])


def split_exchange(x, even_mask, odd_mask):
    size = lax.axis_size("pairs")
    return lax.ppermute(x, "pairs", [(i, i ^ (odd_mask if i & 1 else even_mask)) for i in range(size)])


def in_order(odd, own, partner):
    return jnp.where(odd, jnp.stack([partner, own]), jnp.stack([own, partner]))


def lane_cumsum(x):
    width = x.shape[1]
    lane = lax.broadcasted_iota(jnp.int32, x.shape, 1)
    step = 1
    while step < width:
        x = x + jnp.where(lane >= step, pltpu.roll(x, step, 1), 0)
        step *= 2
    return x


def lookup(table_ref, index):
    value = jnp.zeros(index.shape, F32)
    for part in range(table_ref.shape[0]):
        row = jnp.broadcast_to(table_ref[part : part + 1, :], index.shape)
        near = jnp.clip(index - 128 * part, 0, 127)
        found = jnp.take_along_axis(row, near, axis=1)
        value = jnp.where(index // 128 == part, found, value)
    return value


def load_kernel(n, me_ref, map_hbm, val_hbm, screen_hbm, scaled_ref, order_ref, screen_ref, map_ref, val_ref, sems):
    rows = val_ref.shape[0]
    per_peer = rows // n
    lanes = rows // 128
    parts = 4
    tall = rows // parts
    first = pl.multiple_of((me_ref[0] // 2) * (2 * lanes), lanes)
    head = [
        pltpu.make_async_copy(screen_hbm, screen_ref, sems.at[0]),
        pltpu.make_async_copy(map_hbm.at[pl.ds(first, 2 * lanes), :], map_ref, sems.at[1]),
    ]
    body = [
        pltpu.make_async_copy(
            val_hbm.at[pl.ds(k * tall, tall), :], val_ref.at[pl.ds(k * tall, tall), :], sems.at[2 + k])
        for k in range(parts)
    ]
    for copy in head + body:
        copy.start()
    for copy in head:
        copy.wait()
    block = lax.broadcasted_iota(jnp.int32, (n, rows), 0)
    for flip in range(2):
        at = pl.multiple_of(((me_ref[0] & 1) ^ flip) * lanes, lanes)
        own = map_ref[pl.ds(at, lanes), :]
        own = jnp.concatenate([own[c : c + 1, :] for c in range(lanes)], axis=1)
        own = jnp.broadcast_to(own, (n, rows))
        goes = (own >= block * rows) & (own < (block + 1) * rows)
        rank = lane_cumsum(goes.astype(jnp.int32)) - 1
        order_ref[flip : flip + 1, :] = jnp.sum(
            jnp.where(goes, rank + block * per_peer, 0), axis=0, keepdims=True)
    for k, copy in enumerate(body):
        copy.wait()
        part = slice(k * tall, (k + 1) * tall)
        scaled_ref[part, :] = (val_ref[part, :].astype(F32) * screen_ref[...]).astype(BF16)


def fetch_kernel(trial_hbm, cond_hbm, trial_ref, cond_ref, sems):
    copies = [
        pltpu.make_async_copy(trial_hbm, trial_ref, sems.at[0]),
        pltpu.make_async_copy(cond_hbm, cond_ref, sems.at[1]),
    ]
    for copy in copies:
        copy.start()
    for copy in copies:
        copy.wait()


def send_order(order, scaled, sent_ref):
    rows = sent_ref.shape[0]
    chunk = 128
    for c in range(rows // chunk):
        ids = lax.broadcasted_iota(jnp.int32, (chunk, rows), 0) + c * chunk
        pick = jnp.where(ids == order, 1.0, 0.0).astype(BF16)
        sent_ref[c * chunk : (c + 1) * chunk, :] = jnp.dot(
            pick, scaled, preferred_element_type=F32
        ).astype(BF16)


def sent_kernel(order_ref, scaled_ref, sent_ref):
    send_order(order_ref[0:1, :], scaled_ref[...], sent_ref)


def other_kernel(parity, me_ref, order_ref, screen_ref, val_ref, *refs):
    @pl.when((me_ref[0] & 1) == parity)
    def _():
        scaled = (val_ref[...].astype(F32) * screen_ref[...]).astype(BF16)
        send_order(order_ref[1:2, :], scaled, refs[-1])


def place_kernel(n, rows, me_ref, map_ref, ci_ref, vi_ref, ce_ref, ve_ref, slot_ref, gap_ref):
    per_peer = rows // n
    lanes = rows // 128
    gap_ref[...] = lookup(ce_ref, ci_ref[...]) - lookup(ve_ref, vi_ref[...])
    grid = jnp.concatenate([map_ref[pl.ds(c, n, stride=lanes), :] for c in range(lanes)], axis=1)
    slots = grid - me_ref[0] * rows
    lands = (slots >= 0) & (slots < rows)
    arrival = jnp.where(lands, lane_cumsum(lands.astype(jnp.int32)) - 1, -1)
    slots = slots.astype(F32)
    ids = lax.broadcasted_iota(jnp.int32, (per_peer, rows), 0)
    for q in range(n):
        hit = ids == arrival[q : q + 1, :]
        slot = jnp.sum(jnp.where(hit, slots[q : q + 1, :], 0.0), axis=1, keepdims=True)
        slot_ref[q * per_peer : (q + 1) * per_peer, :] = jnp.broadcast_to(slot, (per_peer, 128))


def tile_kernel(me_ref, val_ref, screen_ref, mine_ref, theirs_ref, out_ref):
    scaled = (val_ref[...].astype(F32) * screen_ref[...]).astype(BF16)
    chips, cols, _ = mine_ref.shape
    me = me_ref[0]
    for k in range(chips):
        for flip, cond_ref in enumerate((mine_ref, theirs_ref)):
            tile = lax.dot_general(
                scaled, cond_ref[k], (((1,), (1,)), ((), ())), preferred_element_type=F32
            )
            start = pl.multiple_of((me ^ (2 * k + flip)) * cols, 128)
            out_ref[0, :, pl.ds(start, cols)] = tile.astype(BF16)


def mixed_kernel(m, me_ref, vec_ref, cond_ref, keep_ref, give_ref):
    chips, vecs, cols = vec_ref.shape
    depth = cond_ref.shape[-1]
    odd = (me_ref[0] & 1) == 1
    vec = jnp.concatenate([vec_ref[k] for k in range(chips)], axis=1)
    total = jnp.dot(vec, cond_ref[...].reshape(chips * cols, depth), preferred_element_type=F32)
    half = vecs // (2 * m)
    for k in range(m):
        low = total[2 * k * half : (2 * k + 1) * half]
        high = total[(2 * k + 1) * half : (2 * k + 2) * half]
        keep_ref[k * half : (k + 1) * half, :] = jnp.where(odd, high, low)
        give_ref[k * half : (k + 1) * half, :] = jnp.where(odd, low, high).astype(BF16)


def apply_kernel(m, n, me_ref, keep_ref, take_ref, own_ref, other_ref, out_hbm, out_ref, sems):
    half, width = out_ref.shape[1:]
    per_peer = width // 2
    odd = (me_ref[0] & 1) == 1
    mixed = (keep_ref[...] + take_ref[...].astype(F32)).astype(BF16)
    shares = sems.shape[0]
    tall = own_ref.shape[0] // shares
    blocks = (n // shares) * m
    copies = []
    for share in range(shares):
        part = slice(share * tall, (share + 1) * tall)
        own, other = (
            lax.dot_general(
                mixed, ref[part, :], (((1,), (1,)), ((), ())), preferred_element_type=F32
            ).astype(BF16)
            for ref in (own_ref, other_ref)
        )
        first, second = jnp.where(odd, other, own), jnp.where(odd, own, other)
        for d in range(n // shares):
            at = slice(d * per_peer, (d + 1) * per_peer)
            for k in range(m):
                to = share * blocks + d * m + k
                out_ref[to, :, :per_peer] = first[k * half : (k + 1) * half, at]
                out_ref[to, :, per_peer:] = second[k * half : (k + 1) * half, at]
        some = pl.ds(share * blocks, blocks)
        copies.append(pltpu.make_async_copy(out_ref.at[some], out_hbm.at[some], sems.at[share]))
        copies[-1].start()
    for copy in copies:
        copy.wait()


def final_kernel(n, m, arrived_ref, slot_ref, gap_ref, trial_ref, out_ref, row_ref):
    width = out_ref.shape[1]
    half, pair = arrived_ref.shape[1:]
    for q in range(n):
        total = arrived_ref[q * m].astype(F32)
        for k in range(1, m):
            total = total + arrived_ref[q * m + k].astype(F32)
        at = (q & 1) * half
        row_ref[at : at + half, (q // 2) * pair : (q // 2 + 1) * pair] = total.astype(BF16)
    slot = slot_ref[...]
    lane = lax.broadcasted_iota(jnp.int32, slot.shape, 1).astype(F32)
    for c in range(0, width // 128, 2):
        lands = jnp.concatenate(
            [jnp.where(slot == lane + 128.0 * (c + k), 1.0, 0.0).astype(BF16) for k in range(2)], axis=1)
        moved = jnp.dot(row_ref[...], lands, preferred_element_type=F32)
        for k in range(2):
            part = slice((c + k) * 128, (c + k + 1) * 128)
            gap = gap_ref[c + k : c + k + 1, :]
            out_ref[:, part] = (
                gap * trial_ref[:, part].astype(F32) + moved[:, k * 128 : (k + 1) * 128]
            ).astype(BF16)


def per_device(
    mat_val,
    mat_cond,
    screening,
    trial_cols,
    trial_rows,
    row_map,
    val_index,
    cond_index,
    val_energy,
    cond_energy,
):
    n = lax.axis_size("pairs")
    m = lax.axis_size("rep")
    rows, depth = mat_val.shape
    cols = mat_cond.shape[0]
    vecs = trial_cols.shape[1]
    half = vecs // 2
    per_peer = rows // n
    own = lax.axis_index("pairs").astype(jnp.int32)
    layer = lax.axis_index("rep").astype(jnp.int32)
    odd = (own & 1) == 1
    me = own.reshape(1)
    screen = screening.reshape(1, depth)
    map_lanes = row_map.reshape(-1, 128)

    far_away = pl.BlockSpec(memory_space=pltpu.HBM)

    def in_hbm(x):
        return pltpu.with_memory_space_constraint(x, pltpu.HBM)

    val_other = exchange(mat_val, 1)
    trial, cond_own = pl.pallas_call(
        fetch_kernel,
        in_specs=[far_away, far_away],
        out_specs=(WHOLE, WHOLE),
        out_shape=(
            jax.ShapeDtypeStruct((vecs, cols), BF16),
            jax.ShapeDtypeStruct((cols, depth), BF16),
        ),
        scratch_shapes=[pltpu.SemaphoreType.DMA((2,))],
        cost_estimate=pl.CostEstimate(flops=0, bytes_accessed=4 * cols * depth, transcendentals=0),
        compiler_params=roomy(4),
        name="fetch",
    )(in_hbm(trial_cols.T), in_hbm(mat_cond))
    turns = [trial]
    for k in range(1, m):
        turns.append(lax.ppermute(trial_cols.T, "rep", [(i, (i + k) % m) for i in range(m)]))
    wide = []
    for k in range(m):
        block = turns[0]
        for t in range(1, m):
            block = jnp.where(lax.rem(layer - t + m, m) == k, turns[t], block)
        wide.append(block)
    wide = jnp.concatenate(wide)
    vec_all = jnp.stack([wide] + [exchange(wide, k) for k in range(2, n, 2)])
    if n == 8:
        near = split_exchange(mat_cond, 2, 4)
        far = split_exchange(jnp.stack([cond_own, near]), 4, 2)
        mine = jnp.stack([cond_own, jnp.where(odd, far[0], near), jnp.where(odd, near, far[0]), far[1]])
    else:
        mine = jnp.stack([cond_own] + [exchange(mat_cond, k) for k in range(2, n, 2)])
    theirs = exchange(mine, 1)
    scaled, order, screen_near = pl.pallas_call(
        lambda *refs: load_kernel(n, *refs),
        in_specs=[SCALAR] + [far_away] * 3,
        out_specs=(WHOLE, WHOLE, WHOLE),
        out_shape=(
            jax.ShapeDtypeStruct((rows, depth), BF16),
            jax.ShapeDtypeStruct((2, rows), jnp.int32),
            jax.ShapeDtypeStruct((1, depth), F32),
        ),
        scratch_shapes=[
            pltpu.VMEM((2 * rows // 128, 128), jnp.int32),
            pltpu.VMEM((rows, depth), BF16),
            pltpu.SemaphoreType.DMA((6,)),
        ],
        cost_estimate=pl.CostEstimate(flops=rows * depth, bytes_accessed=4 * rows * depth, transcendentals=0),
        compiler_params=roomy(8),
        name="load",
    )(me, in_hbm(map_lanes), in_hbm(mat_val), in_hbm(screen))
    sent_cost = pl.CostEstimate(
        flops=2 * rows * rows * depth, bytes_accessed=4 * rows * depth, transcendentals=0)
    sent_shape = jax.ShapeDtypeStruct((rows, depth), BF16)
    sent = pl.pallas_call(
        sent_kernel,
        in_specs=[WHOLE] * 2,
        out_specs=WHOLE,
        out_shape=sent_shape,
        cost_estimate=sent_cost,
        compiler_params=roomy(6),
        name="sent0",
    )(order, scaled)
    sent_other = ()
    for parity in (1, 0):
        sent_other = (pl.pallas_call(
            lambda *refs, parity=parity: other_kernel(parity, *refs),
            in_specs=[SCALAR] + [WHOLE] * (3 + len(sent_other)),
            out_specs=WHOLE,
            out_shape=sent_shape,
            input_output_aliases={4: 0} if sent_other else {},
            cost_estimate=sent_cost,
            compiler_params=roomy(6),
        )(me, order, screen_near, val_other, *sent_other),)
    sent = (sent, *sent_other)
    keep, give = pl.pallas_call(
        lambda *refs: mixed_kernel(m, *refs),
        in_specs=[SCALAR, WHOLE, WHOLE],
        out_specs=(WHOLE, WHOLE),
        out_shape=(
            jax.ShapeDtypeStruct((m * half, depth), F32),
            jax.ShapeDtypeStruct((m * half, depth), BF16),
        ),
        cost_estimate=pl.CostEstimate(
            flops=2 * m * vecs * n * cols * depth // 2, bytes_accessed=n * cols * depth, transcendentals=0),
        compiler_params=roomy(8),
        name="mixed",
    )(me, vec_all, mine)
    take = exchange(give, 1)

    if per_peer % 128 == 0:
        outgoing = pl.pallas_call(
            lambda *refs: apply_kernel(m, n, *refs),
            in_specs=[SCALAR] + [WHOLE] * 4,
            out_specs=pl.BlockSpec(memory_space=pltpu.HBM),
            scratch_shapes=[
                pltpu.VMEM((n * m, half, 2 * per_peer), BF16),
                pltpu.SemaphoreType.DMA((2,)),
            ],
            compiler_params=roomy(8),
            out_shape=jax.ShapeDtypeStruct((n * m, half, 2 * per_peer), BF16),
            cost_estimate=pl.CostEstimate(
                flops=4 * rows * depth * m * half, bytes_accessed=4 * rows * depth, transcendentals=0),
            name="apply",
        )(me, keep, take, *sent)
    else:
        mixed = (keep + take.astype(F32)).astype(BF16)
        partial = jnp.einsum("vg,srg->svr", mixed, jnp.stack(sent), preferred_element_type=F32).astype(BF16)
        partial = in_order(odd, partial[0], partial[1]).reshape(2, m, half, n, per_peer)
        outgoing = partial.transpose(3, 1, 2, 0, 4).reshape(n * m, half, 2 * per_peer)
    arrived = lax.all_to_all(outgoing, ("pairs", "rep"), split_axis=0, concat_axis=0, tiled=True)

    tall = min(rows, 256)
    tiles = pl.pallas_call(
        tile_kernel,
        grid_spec=pltpu.PrefetchScalarGridSpec(
            num_scalar_prefetch=1,
            grid=(rows // tall,),
            in_specs=[
                pl.BlockSpec((tall, depth), lambda d, me: (d, 0)),
                pl.BlockSpec((1, depth), lambda d, me: (0, 0)),
                pl.BlockSpec((n // 2, cols, depth), lambda d, me: (0, 0, 0)),
                pl.BlockSpec((n // 2, cols, depth), lambda d, me: (0, 0, 0)),
            ],
            out_specs=pl.BlockSpec((1, tall, n * cols), lambda d, me: (0, d, 0)),
        ),
        out_shape=jax.ShapeDtypeStruct((1, rows, n * cols), BF16),
        cost_estimate=pl.CostEstimate(
            flops=2 * rows * depth * n * cols, bytes_accessed=2 * rows * (depth + n * cols), transcendentals=0),
        compiler_params=roomy(8),
        name="tiles",
    )(me, mat_val, screen, mine, theirs)

    slot, gap = pl.pallas_call(
        lambda *refs: place_kernel(n, rows, *refs),
        in_specs=[SCALAR] + [WHOLE] * 5,
        out_specs=(WHOLE, WHOLE),
        out_shape=(
            jax.ShapeDtypeStruct((rows, 128), F32),
            jax.ShapeDtypeStruct((rows // 128, 128), F32),
        ),
        cost_estimate=pl.CostEstimate(
            flops=8 * rows * rows, bytes_accessed=2 * rows * rows, transcendentals=0),
        compiler_params=roomy(8),
        name="place",
    )(
        me,
        map_lanes,
        cond_index.reshape(-1, 128),
        val_index.reshape(-1, 128),
        cond_energy.reshape(-1, 128),
        val_energy.reshape(-1, 128),
    )

    if per_peer % 128 != 0:
        arrived = jnp.sum(arrived.reshape(n // 2, 2, m, half, 2 * per_peer).astype(F32), axis=2).astype(BF16)
        arrived = arrived.transpose(1, 2, 0, 3).reshape(2, half, rows)
    parts, layers = (n, m) if per_peer % 128 == 0 else (2, 1)
    response = pl.pallas_call(
        lambda *refs: final_kernel(parts, layers, *refs),
        in_specs=[WHOLE] * 4,
        out_specs=WHOLE,
        compiler_params=roomy(8),
        out_shape=jax.ShapeDtypeStruct((vecs, rows), BF16),
        scratch_shapes=[pltpu.VMEM((vecs, rows), BF16)],
        cost_estimate=pl.CostEstimate(
            flops=2 * rows * rows * vecs, bytes_accessed=2 * rows * rows, transcendentals=0),
        name="final",
    )(arrived, slot, gap, trial_rows.T)
    return (response.T, tiles)


def solution(mesh):
    in_specs = (
        P("pairs", "rep"),
        P("pairs", "rep"),
        P("rep"),
        P("pairs", "rep"),
        P("pairs", "rep"),
        P(),
        P("pairs"),
        P("pairs"),
        P(),
        P(),
    )
    out_specs = (P("pairs", "rep"), P("rep", "pairs", None))

    return jax.shard_map(per_device, mesh=mesh, in_specs=in_specs, out_specs=out_specs, check_vma=False)
```

```python
import jax
import jax.numpy as jnp
from jax import lax
from jax.experimental import pallas as pl
from jax.experimental.pallas import tpu as pltpu
from jax.sharding import PartitionSpec as P

F32 = jnp.float32
BF16 = jnp.bfloat16
SCALAR = pl.BlockSpec(memory_space=pltpu.SMEM)
WHOLE = pl.BlockSpec(memory_space=pltpu.VMEM)


def roomy(mib):
    return pltpu.CompilerParams(vmem_limit_bytes=mib << 20)


def exchange(x, mask):
    size = lax.axis_size("pairs")
    return lax.ppermute(x, "pairs", [(i, i ^ mask) for i in range(size)])


def split_exchange(x, even_mask, odd_mask):
    size = lax.axis_size("pairs")
    return lax.ppermute(x, "pairs", [(i, i ^ (odd_mask if i & 1 else even_mask)) for i in range(size)])


def in_order(odd, own, partner):
    return jnp.where(odd, jnp.stack([partner, own]), jnp.stack([own, partner]))


def lane_cumsum(x):
    width = x.shape[1]
    lane = lax.broadcasted_iota(jnp.int32, x.shape, 1)
    step = 1
    while step < width:
        x = x + jnp.where(lane >= step, pltpu.roll(x, step, 1), 0)
        step *= 2
    return x


def lookup(table_ref, index):
    value = jnp.zeros(index.shape, F32)
    for part in range(table_ref.shape[0]):
        row = jnp.broadcast_to(table_ref[part : part + 1, :], index.shape)
        near = jnp.clip(index - 128 * part, 0, 127)
        found = jnp.take_along_axis(row, near, axis=1)
        value = jnp.where(index // 128 == part, found, value)
    return value


def load_kernel(n, me_ref, map_hbm, val_hbm, screen_hbm, scaled_ref, order_ref, screen_ref, map_ref, val_ref, sems):
    rows = val_ref.shape[0]
    per_peer = rows // n
    lanes = rows // 128
    parts = 4
    tall = rows // parts
    first = pl.multiple_of((me_ref[0] // 2) * (2 * lanes), lanes)
    head = [
        pltpu.make_async_copy(screen_hbm, screen_ref, sems.at[0]),
        pltpu.make_async_copy(map_hbm.at[pl.ds(first, 2 * lanes), :], map_ref, sems.at[1]),
    ]
    body = [
        pltpu.make_async_copy(
            val_hbm.at[pl.ds(k * tall, tall), :], val_ref.at[pl.ds(k * tall, tall), :], sems.at[2 + k])
        for k in range(parts)
    ]
    for copy in head + body:
        copy.start()
    for copy in head:
        copy.wait()
    block = lax.broadcasted_iota(jnp.int32, (n, rows), 0)
    for flip in range(2):
        at = pl.multiple_of(((me_ref[0] & 1) ^ flip) * lanes, lanes)
        own = map_ref[pl.ds(at, lanes), :]
        own = jnp.concatenate([own[c : c + 1, :] for c in range(lanes)], axis=1)
        own = jnp.broadcast_to(own, (n, rows))
        goes = (own >= block * rows) & (own < (block + 1) * rows)
        rank = lane_cumsum(goes.astype(jnp.int32)) - 1
        order_ref[flip : flip + 1, :] = jnp.sum(
            jnp.where(goes, rank + block * per_peer, 0), axis=0, keepdims=True)
    for k, copy in enumerate(body):
        copy.wait()
        part = slice(k * tall, (k + 1) * tall)
        scaled_ref[part, :] = (val_ref[part, :].astype(F32) * screen_ref[...]).astype(BF16)


def fetch_kernel(trial_hbm, cond_hbm, trial_ref, cond_ref, sems):
    copies = [
        pltpu.make_async_copy(trial_hbm, trial_ref, sems.at[0]),
        pltpu.make_async_copy(cond_hbm, cond_ref, sems.at[1]),
    ]
    for copy in copies:
        copy.start()
    for copy in copies:
        copy.wait()


def send_order(order, scaled, sent_ref):
    rows = sent_ref.shape[0]
    chunk = 128
    for c in range(rows // chunk):
        ids = lax.broadcasted_iota(jnp.int32, (chunk, rows), 0) + c * chunk
        pick = jnp.where(ids == order, 1.0, 0.0).astype(BF16)
        sent_ref[c * chunk : (c + 1) * chunk, :] = jnp.dot(
            pick, scaled, preferred_element_type=F32
        ).astype(BF16)


def sent_kernel(order_ref, scaled_ref, sent_ref):
    send_order(order_ref[0:1, :], scaled_ref[...], sent_ref)


def other_kernel(parity, me_ref, order_ref, screen_ref, val_ref, *refs):
    @pl.when((me_ref[0] & 1) == parity)
    def _():
        scaled = (val_ref[...].astype(F32) * screen_ref[...]).astype(BF16)
        send_order(order_ref[1:2, :], scaled, refs[-1])


def place_kernel(n, rows, me_ref, map_ref, ci_ref, vi_ref, ce_ref, ve_ref, trial_ref, slot_ref, base_ref):
    per_peer = rows // n
    lanes = rows // 128
    gap = lookup(ce_ref, ci_ref[...]) - lookup(ve_ref, vi_ref[...])
    for c in range(lanes):
        part = slice(c * 128, (c + 1) * 128)
        base_ref[:, part] = gap[c : c + 1, :] * trial_ref[:, part].astype(F32)
    grid = jnp.concatenate([map_ref[pl.ds(c, n, stride=lanes), :] for c in range(lanes)], axis=1)
    slots = grid - me_ref[0] * rows
    lands = (slots >= 0) & (slots < rows)
    arrival = jnp.where(lands, lane_cumsum(lands.astype(jnp.int32)) - 1, -1)
    slots = slots.astype(F32)
    ids = lax.broadcasted_iota(jnp.int32, (per_peer, rows), 0)
    for q in range(n):
        hit = ids == arrival[q : q + 1, :]
        slot = jnp.sum(jnp.where(hit, slots[q : q + 1, :], 0.0), axis=1, keepdims=True)
        slot_ref[q * per_peer : (q + 1) * per_peer, :] = jnp.broadcast_to(slot, (per_peer, 128))


def tile_kernel(me_ref, val_ref, screen_ref, mine_ref, theirs_ref, out_ref):
    scaled = (val_ref[...].astype(F32) * screen_ref[...]).astype(BF16)
    chips, cols, _ = mine_ref.shape
    me = me_ref[0]
    for k in range(chips):
        for flip, cond_ref in enumerate((mine_ref, theirs_ref)):
            tile = lax.dot_general(
                scaled, cond_ref[k], (((1,), (1,)), ((), ())), preferred_element_type=F32
            )
            start = pl.multiple_of((me ^ (2 * k + flip)) * cols, 128)
            out_ref[0, :, pl.ds(start, cols)] = tile.astype(BF16)


def mixed_kernel(m, me_ref, vec_ref, cond_ref, keep_ref, give_ref):
    chips, vecs, cols = vec_ref.shape
    depth = cond_ref.shape[-1]
    odd = (me_ref[0] & 1) == 1
    vec = jnp.concatenate([vec_ref[k] for k in range(chips)], axis=1)
    total = jnp.dot(vec, cond_ref[...].reshape(chips * cols, depth), preferred_element_type=F32)
    half = vecs // (2 * m)
    for k in range(m):
        low = total[2 * k * half : (2 * k + 1) * half]
        high = total[(2 * k + 1) * half : (2 * k + 2) * half]
        keep_ref[k * half : (k + 1) * half, :] = jnp.where(odd, high, low)
        give_ref[k * half : (k + 1) * half, :] = jnp.where(odd, low, high).astype(BF16)


def apply_kernel(m, n, me_ref, keep_ref, take_ref, own_ref, other_ref, out_hbm, out_ref, sems):
    half, width = out_ref.shape[1:]
    per_peer = width // 2
    odd = (me_ref[0] & 1) == 1
    mixed = (keep_ref[...] + take_ref[...].astype(F32)).astype(BF16)
    shares = sems.shape[0]
    tall = own_ref.shape[0] // shares
    blocks = (n // shares) * m
    copies = []
    for share in range(shares):
        part = slice(share * tall, (share + 1) * tall)
        own, other = (
            lax.dot_general(
                mixed, ref[part, :], (((1,), (1,)), ((), ())), preferred_element_type=F32
            ).astype(BF16)
            for ref in (own_ref, other_ref)
        )
        first, second = jnp.where(odd, other, own), jnp.where(odd, own, other)
        for d in range(n // shares):
            at = slice(d * per_peer, (d + 1) * per_peer)
            for k in range(m):
                to = share * blocks + d * m + k
                out_ref[to, :, :per_peer] = first[k * half : (k + 1) * half, at]
                out_ref[to, :, per_peer:] = second[k * half : (k + 1) * half, at]
        some = pl.ds(share * blocks, blocks)
        copies.append(pltpu.make_async_copy(out_ref.at[some], out_hbm.at[some], sems.at[share]))
        copies[-1].start()
    for copy in copies:
        copy.wait()


def final_kernel(n, m, arrived_ref, slot_ref, base_ref, out_hbm, row_ref, out_ref, sems):
    width = out_ref.shape[1]
    half, pair = arrived_ref.shape[1:]
    for q in range(n):
        total = arrived_ref[q * m].astype(F32)
        for k in range(1, m):
            total = total + arrived_ref[q * m + k].astype(F32)
        at = (q & 1) * half
        row_ref[at : at + half, (q // 2) * pair : (q // 2 + 1) * pair] = total.astype(BF16)
    copies = []
    slot = slot_ref[...]
    lane = lax.broadcasted_iota(jnp.int32, slot.shape, 1).astype(F32)
    for c in range(0, width // 128, 2):
        lands = jnp.concatenate(
            [jnp.where(slot == lane + 128.0 * (c + k), 1.0, 0.0).astype(BF16) for k in range(2)], axis=1)
        moved = jnp.dot(row_ref[...], lands, preferred_element_type=F32)
        part = pl.ds(c * 128, 256)
        out_ref[:, part] = (base_ref[:, part] + moved).astype(BF16)
        copies.append(pltpu.make_async_copy(out_ref.at[:, part], out_hbm.at[:, part], sems.at[c // 2]))
        copies[-1].start()
    for copy in copies:
        copy.wait()


def per_device(
    mat_val,
    mat_cond,
    screening,
    trial_cols,
    trial_rows,
    row_map,
    val_index,
    cond_index,
    val_energy,
    cond_energy,
):
    n = lax.axis_size("pairs")
    m = lax.axis_size("rep")
    rows, depth = mat_val.shape
    cols = mat_cond.shape[0]
    vecs = trial_cols.shape[1]
    half = vecs // 2
    per_peer = rows // n
    own = lax.axis_index("pairs").astype(jnp.int32)
    layer = lax.axis_index("rep").astype(jnp.int32)
    odd = (own & 1) == 1
    me = own.reshape(1)
    screen = screening.reshape(1, depth)
    map_lanes = row_map.reshape(-1, 128)

    far_away = pl.BlockSpec(memory_space=pltpu.HBM)

    def in_hbm(x):
        return pltpu.with_memory_space_constraint(x, pltpu.HBM)

    val_other = exchange(mat_val, 1)
    trial, cond_own = pl.pallas_call(
        fetch_kernel,
        in_specs=[far_away, far_away],
        out_specs=(WHOLE, WHOLE),
        out_shape=(
            jax.ShapeDtypeStruct((vecs, cols), BF16),
            jax.ShapeDtypeStruct((cols, depth), BF16),
        ),
        scratch_shapes=[pltpu.SemaphoreType.DMA((2,))],
        cost_estimate=pl.CostEstimate(flops=0, bytes_accessed=4 * cols * depth, transcendentals=0),
        compiler_params=roomy(4),
        name="fetch",
    )(in_hbm(trial_cols.T), in_hbm(mat_cond))
    turns = [trial]
    for k in range(1, m):
        turns.append(lax.ppermute(trial_cols.T, "rep", [(i, (i + k) % m) for i in range(m)]))
    wide = []
    for k in range(m):
        block = turns[0]
        for t in range(1, m):
            block = jnp.where(lax.rem(layer - t + m, m) == k, turns[t], block)
        wide.append(block)
    wide = jnp.concatenate(wide)
    vec_all = jnp.stack([wide] + [exchange(wide, k) for k in range(2, n, 2)])
    if n == 8:
        near = split_exchange(mat_cond, 2, 4)
        far = split_exchange(jnp.stack([cond_own, near]), 4, 2)
        mine = jnp.stack([cond_own, jnp.where(odd, far[0], near), jnp.where(odd, near, far[0]), far[1]])
    else:
        mine = jnp.stack([cond_own] + [exchange(mat_cond, k) for k in range(2, n, 2)])
    theirs = exchange(mine, 1)
    scaled, order, screen_near = pl.pallas_call(
        lambda *refs: load_kernel(n, *refs),
        in_specs=[SCALAR] + [far_away] * 3,
        out_specs=(WHOLE, WHOLE, WHOLE),
        out_shape=(
            jax.ShapeDtypeStruct((rows, depth), BF16),
            jax.ShapeDtypeStruct((2, rows), jnp.int32),
            jax.ShapeDtypeStruct((1, depth), F32),
        ),
        scratch_shapes=[
            pltpu.VMEM((2 * rows // 128, 128), jnp.int32),
            pltpu.VMEM((rows, depth), BF16),
            pltpu.SemaphoreType.DMA((6,)),
        ],
        cost_estimate=pl.CostEstimate(flops=rows * depth, bytes_accessed=4 * rows * depth, transcendentals=0),
        compiler_params=roomy(8),
        name="load",
    )(me, in_hbm(map_lanes), in_hbm(mat_val), in_hbm(screen))
    sent_cost = pl.CostEstimate(
        flops=2 * rows * rows * depth, bytes_accessed=4 * rows * depth, transcendentals=0)
    sent_shape = jax.ShapeDtypeStruct((rows, depth), BF16)
    sent = pl.pallas_call(
        sent_kernel,
        in_specs=[WHOLE] * 2,
        out_specs=WHOLE,
        out_shape=sent_shape,
        cost_estimate=sent_cost,
        compiler_params=roomy(6),
        name="sent0",
    )(order, scaled)
    sent_other = ()
    for parity in (1, 0):
        sent_other = (pl.pallas_call(
            lambda *refs, parity=parity: other_kernel(parity, *refs),
            in_specs=[SCALAR] + [WHOLE] * (3 + len(sent_other)),
            out_specs=WHOLE,
            out_shape=sent_shape,
            input_output_aliases={4: 0} if sent_other else {},
            cost_estimate=sent_cost,
            compiler_params=roomy(6),
        )(me, order, screen_near, val_other, *sent_other),)
    sent = (sent, *sent_other)
    keep, give = pl.pallas_call(
        lambda *refs: mixed_kernel(m, *refs),
        in_specs=[SCALAR, WHOLE, WHOLE],
        out_specs=(WHOLE, WHOLE),
        out_shape=(
            jax.ShapeDtypeStruct((m * half, depth), F32),
            jax.ShapeDtypeStruct((m * half, depth), BF16),
        ),
        cost_estimate=pl.CostEstimate(
            flops=2 * m * vecs * n * cols * depth // 2, bytes_accessed=n * cols * depth, transcendentals=0),
        compiler_params=roomy(8),
        name="mixed",
    )(me, vec_all, mine)
    take = exchange(give, 1)

    if per_peer % 128 == 0:
        outgoing = pl.pallas_call(
            lambda *refs: apply_kernel(m, n, *refs),
            in_specs=[SCALAR] + [WHOLE] * 4,
            out_specs=pl.BlockSpec(memory_space=pltpu.HBM),
            scratch_shapes=[
                pltpu.VMEM((n * m, half, 2 * per_peer), BF16),
                pltpu.SemaphoreType.DMA((2,)),
            ],
            compiler_params=roomy(8),
            out_shape=jax.ShapeDtypeStruct((n * m, half, 2 * per_peer), BF16),
            cost_estimate=pl.CostEstimate(
                flops=4 * rows * depth * m * half, bytes_accessed=4 * rows * depth, transcendentals=0),
            name="apply",
        )(me, keep, take, *sent)
    else:
        mixed = (keep + take.astype(F32)).astype(BF16)
        partial = jnp.einsum("vg,srg->svr", mixed, jnp.stack(sent), preferred_element_type=F32).astype(BF16)
        partial = in_order(odd, partial[0], partial[1]).reshape(2, m, half, n, per_peer)
        outgoing = partial.transpose(3, 1, 2, 0, 4).reshape(n * m, half, 2 * per_peer)
    arrived = lax.all_to_all(outgoing, ("pairs", "rep"), split_axis=0, concat_axis=0, tiled=True)

    tall = min(rows, 256)
    tiles = pl.pallas_call(
        tile_kernel,
        grid_spec=pltpu.PrefetchScalarGridSpec(
            num_scalar_prefetch=1,
            grid=(rows // tall,),
            in_specs=[
                pl.BlockSpec((tall, depth), lambda d, me: (d, 0)),
                pl.BlockSpec((1, depth), lambda d, me: (0, 0)),
                pl.BlockSpec((n // 2, cols, depth), lambda d, me: (0, 0, 0)),
                pl.BlockSpec((n // 2, cols, depth), lambda d, me: (0, 0, 0)),
            ],
            out_specs=pl.BlockSpec((1, tall, n * cols), lambda d, me: (0, d, 0)),
        ),
        out_shape=jax.ShapeDtypeStruct((1, rows, n * cols), BF16),
        cost_estimate=pl.CostEstimate(
            flops=2 * rows * depth * n * cols, bytes_accessed=2 * rows * (depth + n * cols), transcendentals=0),
        compiler_params=roomy(8),
        name="tiles",
    )(me, mat_val, screen, mine, theirs)

    slot, base = pl.pallas_call(
        lambda *refs: place_kernel(n, rows, *refs),
        in_specs=[SCALAR] + [WHOLE] * 6,
        out_specs=(WHOLE, WHOLE),
        out_shape=(
            jax.ShapeDtypeStruct((rows, 128), F32),
            jax.ShapeDtypeStruct((vecs, rows), F32),
        ),
        cost_estimate=pl.CostEstimate(
            flops=8 * rows * rows, bytes_accessed=2 * rows * rows, transcendentals=0),
        compiler_params=roomy(8),
        name="place",
    )(
        me,
        map_lanes,
        cond_index.reshape(-1, 128),
        val_index.reshape(-1, 128),
        cond_energy.reshape(-1, 128),
        val_energy.reshape(-1, 128),
        trial_rows.T,
    )

    if per_peer % 128 != 0:
        arrived = jnp.sum(arrived.reshape(n // 2, 2, m, half, 2 * per_peer).astype(F32), axis=2).astype(BF16)
        arrived = arrived.transpose(1, 2, 0, 3).reshape(2, half, rows)
    parts, layers = (n, m) if per_peer % 128 == 0 else (2, 1)
    response = pl.pallas_call(
        lambda *refs: final_kernel(parts, layers, *refs),
        in_specs=[WHOLE] * 3,
        out_specs=pl.BlockSpec(memory_space=pltpu.HBM),
        compiler_params=roomy(8),
        out_shape=jax.ShapeDtypeStruct((vecs, rows), BF16),
        scratch_shapes=[
            pltpu.VMEM((vecs, rows), BF16),
            pltpu.VMEM((vecs, rows), BF16),
            pltpu.SemaphoreType.DMA((rows // 256,)),
        ],
        cost_estimate=pl.CostEstimate(
            flops=2 * rows * rows * vecs, bytes_accessed=2 * rows * rows, transcendentals=0),
        name="final",
    )(arrived, slot, base)
    return (response.T, tiles)


def solution(mesh):
    in_specs = (
        P("pairs", "rep"),
        P("pairs", "rep"),
        P("rep"),
        P("pairs", "rep"),
        P("pairs", "rep"),
        P(),
        P("pairs"),
        P("pairs"),
        P(),
        P(),
    )
    out_specs = (P("pairs", "rep"), P("rep", "pairs", None))

    return jax.shard_map(per_device, mesh=mesh, in_specs=in_specs, out_specs=out_specs, check_vma=False)
```
